128 devices in a mesh: gx: 16 (over y, x), gy: 8 (over z, core).
Axes of the slice: x: 4, y: 4, z: 4, core: 2. Of those that a mesh axis runs over, the one named last changes fastest.
Arguments:
- objects: float32 [4, 8192, 4096], P(None, 'gx', 'gy'), may hold values from -3 to 3
- probe_wave: float32 [2, 256, 256], replicated, may hold values from -5 to 5
- prop_phase: float32 [256, 256], replicated, may hold values from -3.140625 to 3.140625
- intensity: float32 [512, 256, 256], P(('gx', 'gy')), may hold values from 0 to 1
- offsets: int32 [512, 2], P(('gx', 'gy')), may hold values from 0 to 512
- counts: int32 [128], P(('gx', 'gy')), may hold values from 1 to 4, 256 in all
Outputs:
- gradient: float32 [4, 8192, 4096], P(None, 'gx', 'gy')
The draws below stay inside these ranges and needn't reach their ends.
Inputs may be any that keep to these rules, and one draw needn't show every extreme that they name: `counts`: every device has at least one live frame; the busiest has exactly 4.
All inputs are finite; a program needn't handle non-finite values.
Results may differ from the reference program's by a relative error of at most 0.00014.
Values sent between devices are 32-bit elements; how exact they have to be, the bound alone decides.
A program may use at most 128 MiB of HBM per device.

```python
import math
import jax
import jax.numpy as jnp
import numpy as np
from jax import lax

FRAME = 256
TILE = 512
CAP = 4
NX = 8192
NY = 4096
SLOTS = 512
N_GY = 8
DEVICES = 128


def plant(drawn, own_key, least, high):
    longest = drawn.shape.index(max(drawn.shape))
    spots = []
    for shift in (0, 1):
        where = [jax.random.randint(jax.random.fold_in(own_key, axis), (), 0, length) for axis, length in enumerate(drawn.shape)]
        where[longest] = (where[longest] + shift) % drawn.shape[longest]
        spots.append(tuple(where))
    return drawn.at[spots[0]].set(least).at[spots[1]].set(high)


def block_levels(key, dims, pieces, smallest, high):
    level = 1.0
    for position, parts in pieces:
        draws = jax.random.uniform(jax.random.fold_in(jax.random.fold_in(key, 6), position), (parts,), jnp.float32, smallest / len(pieces), high / len(pieces))
        level = level * jnp.repeat(jnp.exp(draws), dims[position] // parts).reshape((-1,) + (1,) * (len(dims) - 1 - position))
    return level


def split_up(number_of, total, most, skew):
    loads = [(1 << 20) // math.isqrt(standing ** skew) + 1 for standing in range(2, number_of + 1)]
    spare, holding = total - most - (number_of - 1), [1] * (number_of - 1)
    while spare > 0:
        movable = [i for i in range(number_of - 1) if holding[i] < most]
        mass, budget = sum([loads[i] for i in movable]), spare
        for i in movable:
            extra = min(most - holding[i], max(1, budget * loads[i] // mass), spare)
            holding[i] = holding[i] + extra
            spare = spare - extra
    return np.array([most] + holding)


def ragged(rng, count, total, limit, slope):
    if count == 2:
        one = jax.random.randint(rng, (), max(1, total - limit), min(limit, total - 1) + 1)
        return jnp.stack([one, total - one])
    sizes = jnp.asarray(split_up(count, total, limit, slope), jnp.int32)
    twos = (count - 1) // 2
    giver, taker = sizes[1:1 + 2 * twos:2], sizes[2:2 + 2 * twos:2]
    slack = jnp.minimum(giver - 1, limit - taker)
    shifted = jax.random.randint(jax.random.fold_in(rng, 1), (twos,), 0, 1 << 20) % (slack + 1)
    sizes = sizes.at[1:1 + 2 * twos:2].set(giver - shifted).at[2:2 + 2 * twos:2].set(taker + shifted)
    return sizes[jax.random.permutation(jax.random.fold_in(rng, 2), count)]


def normal_values(own_key, dims, width, bound, pieces=(), kind=jnp.bfloat16):
    result = width * jax.random.normal(own_key, dims, jnp.float32)
    if pieces:
        result = result * block_levels(own_key, dims, pieces, -0.22, 0.18)
    return jnp.clip(result, -bound, bound).astype(kind)


def setup_inputs(seed: int = 0) -> dict:
    seeds = jax.random.split(jax.random.key(seed), 7)
    return {
        "objects": normal_values(seeds[0], (4, NX, NY), 0.5, 3.0, ((1, 16), (2, 8)), jnp.float32),
        "probe_wave": normal_values(seeds[1], (2, FRAME, FRAME), 1.0, 5.0, (), jnp.float32),
        "prop_phase": jnp.clip(jax.random.uniform(seeds[2], (FRAME, FRAME), jnp.float32, -3.140625, 3.140625), -3.140625, 3.140625),
        "intensity": jnp.clip(1.0 * jax.random.uniform(seeds[3], (SLOTS, FRAME, FRAME), jnp.float32) ** block_levels(seeds[3], (SLOTS, FRAME, FRAME), ((0, 128),), -0.2, 0.2), 0.0, 1.0),
        "offsets": plant(jax.random.randint(seeds[4], (SLOTS, 2), 0, TILE + 1), jax.random.fold_in(seeds[4], 1), 0, TILE).astype(jnp.int32),
        "counts": ragged(seeds[5], DEVICES, DEVICES * CAP // 2, CAP, 2).astype(jnp.int32),
    }


def frame_gradient(window, measured, probe_field, propagator):
    slice_one = window[0] + 1j * window[1]
    slice_two = window[2] + 1j * window[3]
    entrance = probe_field * slice_one
    carried = jnp.fft.ifft2(propagator * jnp.fft.fft2(entrance, norm="ortho"), norm="ortho")
    exit_wave = carried * slice_two
    farfield = jnp.fft.fft2(exit_wave, norm="ortho")
    misfit = jnp.real(farfield) ** 2 + jnp.imag(farfield) ** 2 - measured
    grad_exit = jnp.fft.ifft2(misfit * farfield, norm="ortho")
    grad_two = jnp.conj(carried) * grad_exit
    grad_carried = jnp.conj(slice_two) * grad_exit
    grad_entrance = jnp.fft.ifft2(jnp.conj(propagator) * jnp.fft.fft2(grad_carried, norm="ortho"), norm="ortho")
    grad_one = jnp.conj(probe_field) * grad_entrance
    stacked = jnp.stack([jnp.real(grad_one), jnp.imag(grad_one), jnp.real(grad_two), jnp.imag(grad_two)])
    return stacked.astype(window.dtype)


def reference(objects, probe_wave, prop_phase, intensity, offsets, counts):
    margin = FRAME // 2
    padded = jnp.pad(objects, ((0, 0), (margin, margin), (margin, margin)))
    probe_field = probe_wave[0] + 1j * probe_wave[1]
    propagator = jnp.cos(prop_phase) + 1j * jnp.sin(prop_phase)
    slot_ids = jnp.arange(SLOTS, dtype=jnp.int32)
    device_ids = slot_ids // CAP
    row_starts = ((device_ids // N_GY) * TILE + offsets[:, 0]).astype(jnp.int32)
    col_starts = ((device_ids % N_GY) * TILE + offsets[:, 1]).astype(jnp.int32)
    active_slot = (slot_ids % CAP) < counts[device_ids]

    def accumulate(summed, inputs):
        measured, row_start, col_start, active = inputs
        anchor = jnp.int32(0)
        window = lax.dynamic_slice(padded, (anchor, row_start, col_start), (4, FRAME, FRAME))
        update = frame_gradient(window, measured, probe_field, propagator)
        update = jnp.where(active, update, jnp.zeros_like(update))
        current = lax.dynamic_slice(summed, (anchor, row_start, col_start), (4, FRAME, FRAME))
        return lax.dynamic_update_slice(summed, current + update, (anchor, row_start, col_start)), None

    summed, unused = lax.scan(accumulate, jnp.zeros_like(padded), (intensity, row_starts, col_starts, active_slot))
    return summed[:, margin:margin + NX, margin:margin + NY]
```

```python
import functools

import jax
import jax.numpy as jnp
import numpy as np
from jax import lax
from jax.experimental import pallas as pl
from jax.experimental.pallas import tpu as pltpu
from jax.sharding import PartitionSpec as P

F32 = jnp.float32
BF16 = jnp.bfloat16
MESH = pl.DeviceIdType.MESH
CHUNK = 64
COPIES = 14


def phase_tables(frame_len):
    half = frame_len // 2
    n = np.arange(half)[:, None]
    k = np.arange(half)[None, :]
    factor = 1.0 / np.sqrt(frame_len)
    even = 2.0 * np.pi * (n * 2 * k % frame_len) / frame_len
    odd = 2.0 * np.pi * (n * (2 * k + 1) % frame_len) / frame_len
    parts = [np.cos(even), np.sin(even), np.cos(odd), np.sin(odd), np.cos(odd).T, np.sin(odd).T]
    return np.stack([part * factor for part in parts]).astype(np.float32)


def split(value):
    high = value.astype(BF16)
    return high, (value - high.astype(F32)).astype(BF16)


def dot(left, right):
    return jnp.dot(left, right, preferred_element_type=F32)


def times(left_re, left_im, right_re, right_im):
    return left_re * right_re - left_im * right_im, left_re * right_im + left_im * right_re


def conj_times(left_re, left_im, right_re, right_im):
    return left_re * right_re + left_im * right_im, left_re * right_im - left_im * right_re


def kernel(
    n_gx, n_gy, offsets, counts, objects, probe_hbm, phase_hbm, intensity_hbm, tables_hbm, out,
    pad_one, pad_two, place_one, place_two, sum_one, sum_two, rows_one, rows_two, cols_one, cols_two,
    carry, second, gcarry, probe, wave, measured, raw, tables, phase, weights_r, weights_l, rows_in, cols_in,
    send_sem, recv_sem, local_sem, inner_sem,
):
    frame = probe.shape[1]
    half = frame // 2
    cap = intensity_hbm.shape[0]
    tile = objects.shape[1]
    ext = tile + frame
    low, high = half, half + tile
    gx, gy = lax.axis_index("gx"), lax.axis_index("gy")
    has_up, has_down = gx > 0, gx < n_gx - 1
    has_left, has_right = gy > 0, gy < n_gy - 1
    up, down, left, right = (gx - 1, gy), (gx + 1, gy), (gx, gy - 1), (gx, gy + 1)
    slices = ((pad_one, place_one, sum_one, rows_one, cols_one), (pad_two, place_two, sum_two, rows_two, cols_two))

    local = [
        pltpu.make_async_copy(tables_hbm, tables, local_sem.at[0]),
        pltpu.make_async_copy(phase_hbm, phase, local_sem.at[1]),
        pltpu.make_async_copy(intensity_hbm, raw, local_sem.at[2]),
        pltpu.make_async_copy(probe_hbm, probe, local_sem.at[3]),
    ]
    inner = [
        [
            pltpu.make_async_copy(
                objects.at[2 * which : 2 * which + 2, :, block * half : (block + 1) * half],
                pad.at[:, block + 1, low:high],
                inner_sem.at[which, block],
            )
            for block in range(tile // half)
        ]
        for which, pad in enumerate((pad_one, pad_two))
    ]
    local += inner[0] + inner[1]
    for copy in local:
        copy.start()

    barrier = pltpu.get_barrier_semaphore()
    sides = ((has_up, up), (has_down, down), (has_left, left), (has_right, right))
    for there, device in sides:

        @pl.when(there)
        def _():
            pl.semaphore_signal(barrier, inc=1, device_id=device, device_id_type=MESH)

    pl.semaphore_wait(barrier, sum(there.astype(jnp.int32) for there, _ in sides))

    def remote(number, source, target, device, sends, receives):
        copy = pltpu.make_async_remote_copy(
            src_ref=source, dst_ref=target, send_sem=send_sem.at[number], recv_sem=recv_sem.at[number],
            device_id=device, device_id_type=MESH,
        )
        return sends, receives, copy

    def start(copies):
        for sends, _, copy in copies:
            pl.when(sends)(copy.start)

    def wait_recv(copies):
        for _, receives, copy in copies:
            pl.when(receives)(copy.wait_recv)

    def wait_send(copies):
        for sends, _, copy in copies:
            pl.when(sends)(copy.wait_send)

    edge_pieces = (slice(0, half), slice(tile - half, tile))
    middle = slice(half, tile - half)

    def shift_by(piece, distance):
        return slice(piece.start + distance, piece.stop + distance)

    def halo(which):
        pad = slices[which][0]
        cells = objects.at[2 * which : 2 * which + 2]
        base = which * COPIES
        rows = []
        blocks = tile // half
        for block in (0, blocks - 1, *range(1, blocks - 1)):
            piece = slice(block * half, (block + 1) * half)
            rows.append(
                remote(base + len(rows), cells.at[:, 0:half, piece], pad.at[:, block + 1, high:ext], up, has_up, has_down)
            )
            rows.append(
                remote(base + len(rows), cells.at[:, tile - half : tile, piece], pad.at[:, block + 1, 0:low], down, has_down, has_up)
            )
        cols = [
            remote(base + 8, cells.at[:, :, 0:half], pad.at[:, blocks + 1, low:high], left, has_left, has_right),
            remote(base + 9, cells.at[:, :, tile - half : tile], pad.at[:, 0, low:high], right, has_right, has_left),
        ]
        corners = []
        for band, there in ((slice(0, low), has_up), (slice(high, ext), has_down)):
            to_left, to_right = jnp.logical_and(there, has_left), jnp.logical_and(there, has_right)
            corners.append(
                remote(base + 10 + len(corners), pad.at[:, 1, band], pad.at[:, blocks + 1, band], left, to_left, to_right)
            )
            corners.append(
                remote(base + 10 + len(corners), pad.at[:, blocks, band], pad.at[:, 0, band], right, to_right, to_left)
            )
        return rows, cols, corners

    def fold(which):
        _, _, total, land_rows, land_cols = slices[which]
        base = (2 + which) * COPIES
        rows = []
        for piece in (*edge_pieces, middle):
            moved = shift_by(piece, half)
            rows.append(
                remote(base + len(rows), total.at[:, 0:low, moved], land_rows.at[1, :, :, piece], up, has_up, has_down)
            )
            rows.append(
                remote(base + len(rows), total.at[:, high:ext, moved], land_rows.at[0, :, :, piece], down, has_down, has_up)
            )
        cols = [
            remote(base + 6, total.at[:, low:high, 0:low], land_cols.at[1, :, low:high], left, has_left, has_right),
            remote(base + 7, total.at[:, low:high, high:ext], land_cols.at[0, :, low:high], right, has_right, has_left),
        ]
        corners = []
        for band, there in ((slice(0, low), has_up), (slice(high, ext), has_down)):
            to_left, to_right = jnp.logical_and(there, has_left), jnp.logical_and(there, has_right)
            corners.append(
                remote(base + 8 + len(corners), total.at[:, band, 0:low], land_cols.at[1, :, band], left, to_left, to_right)
            )
            corners.append(
                remote(base + 8 + len(corners), total.at[:, band, high:ext], land_cols.at[0, :, band], right, to_right, to_left)
            )
        return rows, cols, corners

    halos = [halo(0), halo(1)]
    folds = [fold(0), fold(1)]

    start(halos[0][0] + halos[0][1])

    for pad in (pad_one, pad_two):

        @pl.when(jnp.logical_not(has_up))
        def _():
            pad[:, :, 0:low] = jnp.zeros((2, ext // half, low, half), F32)

        @pl.when(jnp.logical_not(has_down))
        def _():
            pad[:, :, high:ext] = jnp.zeros((2, ext // half, low, half), F32)

        @pl.when(jnp.logical_not(has_left))
        def _():
            pad[:, 0] = jnp.zeros((2, ext, half), F32)

        @pl.when(jnp.logical_not(has_right))
        def _():
            pad[:, ext // half - 1] = jnp.zeros((2, ext, half), F32)

    local[0].wait()
    cos_e, sin_e, cos_o, sin_o, cos_t, sin_t = (tables[i] for i in range(6))

    def real_form(cosine, sine):
        return jnp.concatenate([jnp.concatenate([cosine, -sine], 1), jnp.concatenate([sine, cosine], 1)], 0)

    forms = (real_form(cos_e, sin_e), real_form(cos_o, sin_o), real_form(cos_e, -sin_e), real_form(cos_t, -sin_t))
    for number, form in enumerate(forms):
        top, rest = split(form)
        for part, value in enumerate((top, top, rest)):
            weights_r[number, part * frame : (part + 1) * frame, :] = value
            weights_l[number, :, part * frame : (part + 1) * frame] = value

    place = lax.broadcasted_iota(jnp.int32, (frame, frame), 0)
    other = lax.broadcasted_iota(jnp.int32, (frame, frame), 1)

    def picked(i):
        return jnp.where(i < half, 2 * i, 2 * (i - half) + 1)

    pick_rows = jnp.where(other == picked(place), 1.0, 0.0).astype(BF16)
    pick_cols = jnp.where(place == picked(other), 1.0, 0.0).astype(BF16)

    def sorted_frequencies(value):
        for axis in (0, 1):
            top, rest = split(value)
            middle_part, last = split(value - top.astype(F32))
            del rest
            parts = (top, middle_part, last)
            if axis == 0:
                value = sum(dot(pick_rows, part) for part in parts[::-1])
            else:
                value = sum(dot(part, pick_cols) for part in parts[::-1])
        return value

    local[1].wait()
    angle = sorted_frequencies(phase[...])
    wave[0] = jnp.cos(angle)
    wave[1] = jnp.sin(angle)
    local[2].wait()

    def sort_slot(slot, nothing):
        measured[slot] = sorted_frequencies(raw[slot])
        return nothing

    lax.fori_loop(0, cap, sort_slot, 0)

    def clear_place(slot, nothing):
        for target in (place_one, place_two):
            for comp in range(2):
                target[comp, slot, 3] = jnp.zeros((4 * half, half), F32)
                for block in range(3):
                    target[comp, slot, block, 0:half] = jnp.zeros((half, half), F32)
                    target[comp, slot, block, 3 * half : 4 * half] = jnp.zeros((half, half), F32)
        return nothing

    lax.fori_loop(0, cap, clear_place, 0)
    local[3].wait()

    lane = lax.broadcasted_iota(jnp.int32, (CHUNK, half), 1)

    def column_of(slot):
        column = offsets[slot, 1]
        block = jnp.minimum(column // half, tile // half - 1)
        return block, column - block * half

    def window(pad, slot, comp, chunk):
        row = offsets[slot, 0]
        block, shift = column_of(slot)
        rows = pl.ds(row + chunk * CHUNK, CHUNK)
        back = jnp.where(jnp.logical_or(shift == 0, shift == half), 0, half - shift)
        turned = [pltpu.roll(pad[comp, block + i, rows, :], back, 1) for i in range(3)]
        kept = lane < half - shift
        return jnp.concatenate([jnp.where(kept, turned[i], turned[i + 1]) for i in range(2)], 1)

    def put(target, slot, comp, chunk, value):
        _, shift = column_of(slot)
        turn = jnp.where(shift == half, 0, shift)
        value = jnp.where(slot < counts[0], value, jnp.zeros_like(value))
        first = pltpu.roll(value[:, :half], turn, 1)
        last = pltpu.roll(value[:, half:], turn, 1)
        inside = lane >= shift
        nothing = jnp.zeros_like(first)
        rows = slice(half + chunk * CHUNK, half + (chunk + 1) * CHUNK)
        target[comp, slot, 0, rows] = jnp.where(inside, first, nothing)
        target[comp, slot, 1, rows] = jnp.where(inside, last, first)
        target[comp, slot, 2, rows] = jnp.where(inside, nothing, last)

    def right_dot(j, number):
        value = rows_in[j]
        return dot(jnp.concatenate([value, value[:, :frame]], 1), weights_r[number])

    def left_dot(i, number):
        value = cols_in[i]
        return dot(weights_l[number], jnp.concatenate([value, value[:frame]], 0))

    def there_and_back(before, between, after):
        chunks = [slice(c * CHUNK, (c + 1) * CHUNK) for c in range(frame // CHUNK)]
        for c, rows in enumerate(chunks):
            re, im = before(c, rows)
            for j in range(2):
                if j == 0:
                    mixed = jnp.concatenate([re[:, :half] + re[:, half:], im[:, :half] + im[:, half:]], 1)
                else:
                    mixed = jnp.concatenate([re[:, :half] - re[:, half:], im[:, :half] - im[:, half:]], 1)
                top, rest = split(mixed)
                rows_in[j, rows, 0:frame] = top
                rows_in[j, rows, frame : 2 * frame] = rest
        for j in range(2):
            value = right_dot(j, j)
            cols = slice(j * half, (j + 1) * half)
            for i in range(2):
                mixed = value[:half] + value[half:] if i == 0 else value[:half] - value[half:]
                for part, piece in enumerate(split(mixed)):
                    cols_in[i, part * frame : part * frame + half, cols] = piece[:, :half]
                    cols_in[i, part * frame + half : (part + 1) * frame, cols] = piece[:, half:]
        for i in range(2):
            value = left_dot(i, 2 + i)
            re, im = between(slice(i * half, (i + 1) * half), value[:half], value[half:])
            for position, field in enumerate((re, im)):
                for part, piece in enumerate(split(field)):
                    begin = part * frame + position * half
                    cols_in[i, begin : begin + half, :] = piece
        even, odd = left_dot(0, 0), left_dot(1, 1)
        for i in range(2):
            mixed = even + odd if i == 0 else even - odd
            rows = slice(i * half, (i + 1) * half)
            for j in range(2):
                for part, piece in enumerate(split(mixed[:, j * half : (j + 1) * half])):
                    begin = part * frame
                    rows_in[j, rows, begin : begin + half] = piece[:half]
                    rows_in[j, rows, begin + half : begin + frame] = piece[half:]
        even, odd = right_dot(0, 2), right_dot(1, 3)
        total, difference = even + odd, even - odd
        for c, rows in enumerate(chunks):
            re = jnp.concatenate([total[rows, :half], difference[rows, :half]], 1)
            im = jnp.concatenate([total[rows, half:], difference[rows, half:]], 1)
            after(c, rows, re, im)

    rows, cols, corners = halos[0]
    wait_recv(rows[:4])
    start(corners)
    wait_recv(rows[4:] + cols)
    start(halos[1][0] + halos[1][1])
    wait_recv(corners)
    for copy in inner[0]:
        copy.wait()

    def enter(slot, nothing):
        def before(chunk, rows):
            return times(probe[0, rows], probe[1, rows], window(pad_one, slot, 0, chunk), window(pad_one, slot, 1, chunk))

        def between(rows, re, im):
            return times(wave[0, rows], wave[1, rows], re, im)

        def after(chunk, rows, re, im):
            carry[slot, 0, rows] = re
            carry[slot, 1, rows] = im

        there_and_back(before, between, after)
        return nothing

    lax.fori_loop(0, cap, enter, 0)

    rows, cols, corners = halos[1]
    wait_recv(rows[:4])
    start(corners)
    wait_recv(rows[4:] + cols + corners)
    for copy in inner[1]:
        copy.wait()

    def leave(slot, nothing):
        def before(chunk, rows):
            second[slot, 0, rows] = window(pad_two, slot, 0, chunk)
            second[slot, 1, rows] = window(pad_two, slot, 1, chunk)
            return times(carry[slot, 0, rows], carry[slot, 1, rows], second[slot, 0, rows], second[slot, 1, rows])

        def between(rows, re, im):
            misfit = re * re + im * im - measured[slot, rows]
            return misfit * re, misfit * im

        def after(chunk, rows, re, im):
            two_re, two_im = conj_times(carry[slot, 0, rows], carry[slot, 1, rows], re, im)
            put(place_two, slot, 0, chunk, two_re)
            put(place_two, slot, 1, chunk, two_im)
            back_re, back_im = conj_times(second[slot, 0, rows], second[slot, 1, rows], re, im)
            gcarry[slot, 0, rows] = back_re
            gcarry[slot, 1, rows] = back_im

        there_and_back(before, between, after)
        return nothing

    lax.fori_loop(0, cap, leave, 0)

    blocks = ext // half

    def gather_block(which, row_block, col_block):
        _, target, total, _, _ = slices[which]
        for comp in range(2):
            value = None
            for slot in range(cap):
                block, _ = column_of(slot)
                moved = col_block - block
                taken = jnp.where(jnp.logical_and(moved >= 0, moved <= 2), moved, 3)
                begin = jnp.clip(row_block * half - offsets[slot, 0] + half, 0, 3 * half)
                piece = target[comp, slot, taken, pl.ds(begin, half), :]
                value = piece if value is None else value + piece
            rows = pl.ds(pl.multiple_of(row_block * half, half), half)
            cols = pl.ds(pl.multiple_of(col_block * half, half), half)
            total[comp, rows, cols] = value

    def gather_rows(which):
        def step(number, nothing):
            gather_block(which, (number // blocks) * (blocks - 1), number % blocks)
            return nothing

        lax.fori_loop(0, 2 * blocks, step, 0)

    def gather_cols(which):
        def step(number, nothing):
            gather_block(which, 1 + number // 2, (number % 2) * (blocks - 1))
            return nothing

        lax.fori_loop(0, 2 * (blocks - 2), step, 0)

    def gather_inner(which):
        def step(number, nothing):
            gather_block(which, 1 + number // (blocks - 2), 1 + number % (blocks - 2))
            return nothing

        lax.fori_loop(0, (blocks - 2) * (blocks - 2), step, 0)

    def send_sums(which):
        rows, cols, corners = folds[which]
        gather_rows(which)
        start(corners + rows[4:])
        gather_cols(which)
        start(cols)
        gather_inner(which)

    def pass_corners(which):
        rows, _, corners = folds[which]
        _, _, total, _, land_cols = slices[which]
        wait_recv(corners)
        for band, there in ((slice(0, low), has_up), (slice(high, ext), has_down)):
            for side, near, cell in ((0, has_left, slice(low, low + half)), (1, has_right, slice(high - half, high))):

                @pl.when(jnp.logical_and(there, near))
                def _():
                    for comp in range(2):
                        total[comp, band, cell] += land_cols[side, comp, band, :]

        start(rows[:4])

    def finish(which):
        rows, cols, corners = folds[which]
        _, _, total, land_rows, land_cols = slices[which]
        wait_recv(cols)
        for side, near, cell in ((0, has_left, slice(low, low + half)), (1, has_right, slice(high - half, high))):

            @pl.when(near)
            def _():
                for comp in range(2):
                    total[comp, low:high, cell] += land_cols[side, comp, low:high, :]

        wait_recv(rows)
        for side, near, cell in ((0, has_up, slice(low, low + half)), (1, has_down, slice(high - half, high))):

            @pl.when(near)
            def _():
                for comp in range(2):
                    total[comp, cell, low:high] += land_rows[side, comp]

        copy = pltpu.make_async_copy(
            total.at[:, low:high, low:high], out.at[2 * which : 2 * which + 2], local_sem.at[6 + which]
        )
        copy.start()
        return copy

    send_sums(1)

    def back(slot, nothing):
        def before(chunk, rows):
            return gcarry[slot, 0, rows], gcarry[slot, 1, rows]

        def between(rows, re, im):
            return conj_times(wave[0, rows], wave[1, rows], re, im)

        def after(chunk, rows, re, im):
            one_re, one_im = conj_times(probe[0, rows], probe[1, rows], re, im)
            put(place_one, slot, 0, chunk, one_re)
            put(place_one, slot, 1, chunk, one_im)

        there_and_back(before, between, after)

        @pl.when(slot == 1)
        def _():
            pass_corners(1)

        return nothing

    lax.fori_loop(0, cap, back, 0)

    send_sums(0)
    last = [finish(1)]
    pass_corners(0)
    last.append(finish(0))
    for exchange in halos + folds:
        for copies in exchange:
            wait_send(copies)
    for copy in last:
        copy.wait()


def shards(n_gx, n_gy, objects, probe_wave, prop_phase, intensity, offsets, counts):
    frame = intensity.shape[1]
    half = frame // 2
    cap = intensity.shape[0]
    tile = objects.shape[1]
    ext = tile + frame
    anywhere = pl.BlockSpec(memory_space=pl.ANY)
    scalars = pl.BlockSpec(memory_space=pltpu.SMEM)
    field = pltpu.VMEM((cap, 2, frame, frame), F32)
    scratch = [
        *[pltpu.VMEM((2, ext // half, ext, half), F32)] * 2,
        *[pltpu.VMEM((2, cap, 4, 4 * half, half), F32)] * 2,
        *[pltpu.VMEM((2, ext, ext), F32)] * 2,
        *[pltpu.VMEM((2, 2, half, tile), F32)] * 2,
        *[pltpu.VMEM((2, 2, ext, half), F32)] * 2,
        field,
        field,
        field,
        pltpu.VMEM((2, frame, frame), F32),
        pltpu.VMEM((2, frame, frame), F32),
        pltpu.VMEM((cap, frame, frame), F32),
        pltpu.VMEM((cap, frame, frame), F32),
        pltpu.VMEM((6, half, half), F32),
        pltpu.VMEM((frame, frame), F32),
        pltpu.VMEM((4, 3 * frame, frame), BF16),
        pltpu.VMEM((4, frame, 3 * frame), BF16),
        pltpu.VMEM((2, frame, 2 * frame), BF16),
        pltpu.VMEM((2, 2 * frame, frame), BF16),
        pltpu.SemaphoreType.DMA((4 * COPIES,)),
        pltpu.SemaphoreType.DMA((4 * COPIES,)),
        pltpu.SemaphoreType.DMA((8,)),
        pltpu.SemaphoreType.DMA((2, tile // half)),
    ]
    return pl.pallas_call(
        functools.partial(kernel, n_gx, n_gy),
        out_shape=jax.ShapeDtypeStruct(objects.shape, F32),
        in_specs=[scalars, scalars, *[anywhere] * 5],
        out_specs=anywhere,
        scratch_shapes=scratch,
        compiler_params=pltpu.CompilerParams(
            collective_id=0, has_side_effects=True, vmem_limit_bytes=60 * 1024 * 1024
        ),
        name="ptychography",
    )(offsets, counts, objects, probe_wave, prop_phase, intensity, jnp.asarray(phase_tables(frame)))


def solution(mesh):
    return jax.shard_map(
        functools.partial(shards, mesh.shape["gx"], mesh.shape["gy"]),
        mesh=mesh,
        in_specs=(
            P(None, "gx", "gy"),
            P(),
            P(),
            P(("gx", "gy"), None, None),
            P(("gx", "gy"), None),
            P(("gx", "gy")),
        ),
        out_specs=P(None, "gx", "gy"),
        check_vma=False,
    )
```

```python
import functools

import jax
import jax.numpy as jnp
import numpy as np
from jax import lax
from jax.experimental import pallas as pl
from jax.experimental.pallas import tpu as pltpu
from jax.sharding import PartitionSpec as P

F32 = jnp.float32
BF16 = jnp.bfloat16
MESH = pl.DeviceIdType.MESH
CHUNK = 64
COPIES = 14


def phase_tables(frame_len):
    half = frame_len // 2
    n = np.arange(half)[:, None]
    k = np.arange(half)[None, :]
    factor = 1.0 / np.sqrt(frame_len)
    even = 2.0 * np.pi * (n * 2 * k % frame_len) / frame_len
    odd = 2.0 * np.pi * (n * (2 * k + 1) % frame_len) / frame_len
    parts = [np.cos(even), np.sin(even), np.cos(odd), np.sin(odd), np.cos(odd).T, np.sin(odd).T]
    return np.stack([part * factor for part in parts]).astype(np.float32)


def split(value):
    high = value.astype(BF16)
    return high, (value - high.astype(F32)).astype(BF16)


def dot(left, right):
    return jnp.dot(left, right, preferred_element_type=F32)


def times(left_re, left_im, right_re, right_im):
    return left_re * right_re - left_im * right_im, left_re * right_im + left_im * right_re


def conj_times(left_re, left_im, right_re, right_im):
    return left_re * right_re + left_im * right_im, left_re * right_im - left_im * right_re


def kernel(
    n_gx, n_gy, offsets_hbm, counts_hbm, objects, probe_hbm, phase_hbm, intensity_hbm, tables_hbm, out,
    pad_one, pad_two, place_one, place_two, sum_one, sum_two, rows_one, rows_two, cols_one, cols_two,
    carry, second, gcarry, probe, wave, measured, raw, tables, phase, weights_r, weights_l, rows_in, cols_in,
    offsets, counts, send_sem, recv_sem, local_sem, inner_sem,
):
    frame = probe.shape[1]
    half = frame // 2
    cap = intensity_hbm.shape[0]
    tile = objects.shape[1]
    ext = tile + frame
    low, high = half, half + tile
    gx, gy = lax.axis_index("gx"), lax.axis_index("gy")
    has_up, has_down = gx > 0, gx < n_gx - 1
    has_left, has_right = gy > 0, gy < n_gy - 1
    up, down, left, right = (gx - 1, gy), (gx + 1, gy), (gx, gy - 1), (gx, gy + 1)
    slices = ((pad_one, place_one, sum_one, rows_one, cols_one), (pad_two, place_two, sum_two, rows_two, cols_two))

    local = [
        pltpu.make_async_copy(tables_hbm, tables, local_sem.at[0]),
        pltpu.make_async_copy(phase_hbm, phase, local_sem.at[1]),
        pltpu.make_async_copy(intensity_hbm, raw, local_sem.at[2]),
        pltpu.make_async_copy(probe_hbm, probe, local_sem.at[3]),
        pltpu.make_async_copy(offsets_hbm, offsets, local_sem.at[4]),
        pltpu.make_async_copy(counts_hbm, counts, local_sem.at[5]),
    ]
    inner = [
        [
            pltpu.make_async_copy(
                objects.at[2 * which : 2 * which + 2, :, block * half : (block + 1) * half],
                pad.at[:, block + 1, low:high],
                inner_sem.at[which, block],
            )
            for block in range(tile // half)
        ]
        for which, pad in enumerate((pad_one, pad_two))
    ]
    local += inner[0] + inner[1]
    for copy in local:
        copy.start()

    barrier = pltpu.get_barrier_semaphore()
    sides = ((has_up, up), (has_down, down), (has_left, left), (has_right, right))
    for there, device in sides:

        @pl.when(there)
        def _():
            pl.semaphore_signal(barrier, inc=1, device_id=device, device_id_type=MESH)

    pl.semaphore_wait(barrier, sum(there.astype(jnp.int32) for there, _ in sides))

    def remote(number, source, target, device, sends, receives):
        copy = pltpu.make_async_remote_copy(
            src_ref=source, dst_ref=target, send_sem=send_sem.at[number], recv_sem=recv_sem.at[number],
            device_id=device, device_id_type=MESH,
        )
        return sends, receives, copy

    def start(copies):
        for sends, _, copy in copies:
            pl.when(sends)(copy.start)

    def wait_recv(copies):
        for _, receives, copy in copies:
            pl.when(receives)(copy.wait_recv)

    def wait_send(copies):
        for sends, _, copy in copies:
            pl.when(sends)(copy.wait_send)

    edge_pieces = (slice(0, half), slice(tile - half, tile))
    middle = slice(half, tile - half)

    def shift_by(piece, distance):
        return slice(piece.start + distance, piece.stop + distance)

    def halo(which):
        pad = slices[which][0]
        cells = objects.at[2 * which : 2 * which + 2]
        base = which * COPIES
        rows = []
        blocks = tile // half
        for block in (0, blocks - 1, *range(1, blocks - 1)):
            piece = slice(block * half, (block + 1) * half)
            rows.append(
                remote(base + len(rows), cells.at[:, 0:half, piece], pad.at[:, block + 1, high:ext], up, has_up, has_down)
            )
            rows.append(
                remote(base + len(rows), cells.at[:, tile - half : tile, piece], pad.at[:, block + 1, 0:low], down, has_down, has_up)
            )
        cols = [
            remote(base + 8, cells.at[:, :, 0:half], pad.at[:, blocks + 1, low:high], left, has_left, has_right),
            remote(base + 9, cells.at[:, :, tile - half : tile], pad.at[:, 0, low:high], right, has_right, has_left),
        ]
        corners = []
        for band, there in ((slice(0, low), has_up), (slice(high, ext), has_down)):
            to_left, to_right = jnp.logical_and(there, has_left), jnp.logical_and(there, has_right)
            corners.append(
                remote(base + 10 + len(corners), pad.at[:, 1, band], pad.at[:, blocks + 1, band], left, to_left, to_right)
            )
            corners.append(
                remote(base + 10 + len(corners), pad.at[:, blocks, band], pad.at[:, 0, band], right, to_right, to_left)
            )
        return rows, cols, corners

    def fold(which):
        _, _, total, land_rows, land_cols = slices[which]
        base = (2 + which) * COPIES
        rows = []
        for piece in (*edge_pieces, middle):
            moved = shift_by(piece, half)
            rows.append(
                remote(base + len(rows), total.at[:, 0:low, moved], land_rows.at[1, :, :, piece], up, has_up, has_down)
            )
            rows.append(
                remote(base + len(rows), total.at[:, high:ext, moved], land_rows.at[0, :, :, piece], down, has_down, has_up)
            )
        cols = [
            remote(base + 6, total.at[:, low:high, 0:low], land_cols.at[1, :, low:high], left, has_left, has_right),
            remote(base + 7, total.at[:, low:high, high:ext], land_cols.at[0, :, low:high], right, has_right, has_left),
        ]
        corners = []
        for band, there in ((slice(0, low), has_up), (slice(high, ext), has_down)):
            to_left, to_right = jnp.logical_and(there, has_left), jnp.logical_and(there, has_right)
            corners.append(
                remote(base + 8 + len(corners), total.at[:, band, 0:low], land_cols.at[1, :, band], left, to_left, to_right)
            )
            corners.append(
                remote(base + 8 + len(corners), total.at[:, band, high:ext], land_cols.at[0, :, band], right, to_right, to_left)
            )
        return rows, cols, corners

    halos = [halo(0), halo(1)]
    folds = [fold(0), fold(1)]

    start(halos[0][0] + halos[0][1])

    for pad in (pad_one, pad_two):

        @pl.when(jnp.logical_not(has_up))
        def _():
            pad[:, :, 0:low] = jnp.zeros((2, ext // half, low, half), F32)

        @pl.when(jnp.logical_not(has_down))
        def _():
            pad[:, :, high:ext] = jnp.zeros((2, ext // half, low, half), F32)

        @pl.when(jnp.logical_not(has_left))
        def _():
            pad[:, 0] = jnp.zeros((2, ext, half), F32)

        @pl.when(jnp.logical_not(has_right))
        def _():
            pad[:, ext // half - 1] = jnp.zeros((2, ext, half), F32)

    local[0].wait()
    cos_e, sin_e, cos_o, sin_o, cos_t, sin_t = (tables[i] for i in range(6))

    def real_form(cosine, sine):
        return jnp.concatenate([jnp.concatenate([cosine, -sine], 1), jnp.concatenate([sine, cosine], 1)], 0)

    forms = (real_form(cos_e, sin_e), real_form(cos_o, sin_o), real_form(cos_e, -sin_e), real_form(cos_t, -sin_t))
    for number, form in enumerate(forms):
        top, rest = split(form)
        for part, value in enumerate((top, top, rest)):
            weights_r[number, part * frame : (part + 1) * frame, :] = value
            weights_l[number, :, part * frame : (part + 1) * frame] = value

    place = lax.broadcasted_iota(jnp.int32, (frame, frame), 0)
    other = lax.broadcasted_iota(jnp.int32, (frame, frame), 1)

    def picked(i):
        return jnp.where(i < half, 2 * i, 2 * (i - half) + 1)

    pick_rows = jnp.where(other == picked(place), 1.0, 0.0).astype(BF16)
    pick_cols = jnp.where(place == picked(other), 1.0, 0.0).astype(BF16)

    def sorted_frequencies(value):
        for axis in (0, 1):
            top, rest = split(value)
            middle_part, last = split(value - top.astype(F32))
            del rest
            parts = (top, middle_part, last)
            if axis == 0:
                value = sum(dot(pick_rows, part) for part in parts[::-1])
            else:
                value = sum(dot(part, pick_cols) for part in parts[::-1])
        return value

    local[1].wait()
    angle = sorted_frequencies(phase[...])
    wave[0] = jnp.cos(angle)
    wave[1] = jnp.sin(angle)
    local[2].wait()

    def sort_slot(slot, nothing):
        measured[slot] = sorted_frequencies(raw[slot])
        return nothing

    lax.fori_loop(0, cap, sort_slot, 0)

    def clear_place(slot, nothing):
        for target in (place_one, place_two):
            for comp in range(2):
                target[comp, slot, 3] = jnp.zeros((4 * half, half), F32)
                for block in range(3):
                    target[comp, slot, block, 0:half] = jnp.zeros((half, half), F32)
                    target[comp, slot, block, 3 * half : 4 * half] = jnp.zeros((half, half), F32)
        return nothing

    lax.fori_loop(0, cap, clear_place, 0)
    local[3].wait()
    local[4].wait()
    local[5].wait()

    lane = lax.broadcasted_iota(jnp.int32, (CHUNK, half), 1)

    def column_of(slot):
        column = offsets[1, slot]
        block = jnp.minimum(column // half, tile // half - 1)
        return block, column - block * half

    def window(pad, slot, comp, chunk):
        row = offsets[0, slot]
        block, shift = column_of(slot)
        rows = pl.ds(row + chunk * CHUNK, CHUNK)
        back = jnp.where(jnp.logical_or(shift == 0, shift == half), 0, half - shift)
        turned = [pltpu.roll(pad[comp, block + i, rows, :], back, 1) for i in range(3)]
        kept = lane < half - shift
        return jnp.concatenate([jnp.where(kept, turned[i], turned[i + 1]) for i in range(2)], 1)

    def put(target, slot, comp, chunk, value):
        _, shift = column_of(slot)
        turn = jnp.where(shift == half, 0, shift)
        value = jnp.where(slot < counts[0], value, jnp.zeros_like(value))
        first = pltpu.roll(value[:, :half], turn, 1)
        last = pltpu.roll(value[:, half:], turn, 1)
        inside = lane >= shift
        nothing = jnp.zeros_like(first)
        rows = slice(half + chunk * CHUNK, half + (chunk + 1) * CHUNK)
        target[comp, slot, 0, rows] = jnp.where(inside, first, nothing)
        target[comp, slot, 1, rows] = jnp.where(inside, last, first)
        target[comp, slot, 2, rows] = jnp.where(inside, nothing, last)

    def right_dot(j, number):
        value = rows_in[j]
        return dot(jnp.concatenate([value, value[:, :frame]], 1), weights_r[number])

    def left_dot(i, number):
        value = cols_in[i]
        return dot(weights_l[number], jnp.concatenate([value, value[:frame]], 0))

    def there_and_back(before, between, after):
        chunks = [slice(c * CHUNK, (c + 1) * CHUNK) for c in range(frame // CHUNK)]
        for c, rows in enumerate(chunks):
            re, im = before(c, rows)
            for j in range(2):
                if j == 0:
                    mixed = jnp.concatenate([re[:, :half] + re[:, half:], im[:, :half] + im[:, half:]], 1)
                else:
                    mixed = jnp.concatenate([re[:, :half] - re[:, half:], im[:, :half] - im[:, half:]], 1)
                top, rest = split(mixed)
                rows_in[j, rows, 0:frame] = top
                rows_in[j, rows, frame : 2 * frame] = rest
        for j in range(2):
            value = right_dot(j, j)
            cols = slice(j * half, (j + 1) * half)
            for i in range(2):
                mixed = value[:half] + value[half:] if i == 0 else value[:half] - value[half:]
                for part, piece in enumerate(split(mixed)):
                    cols_in[i, part * frame : part * frame + half, cols] = piece[:, :half]
                    cols_in[i, part * frame + half : (part + 1) * frame, cols] = piece[:, half:]
        for i in range(2):
            value = left_dot(i, 2 + i)
            re, im = between(slice(i * half, (i + 1) * half), value[:half], value[half:])
            for position, field in enumerate((re, im)):
                for part, piece in enumerate(split(field)):
                    begin = part * frame + position * half
                    cols_in[i, begin : begin + half, :] = piece
        even, odd = left_dot(0, 0), left_dot(1, 1)
        for i in range(2):
            mixed = even + odd if i == 0 else even - odd
            rows = slice(i * half, (i + 1) * half)
            for j in range(2):
                for part, piece in enumerate(split(mixed[:, j * half : (j + 1) * half])):
                    begin = part * frame
                    rows_in[j, rows, begin : begin + half] = piece[:half]
                    rows_in[j, rows, begin + half : begin + frame] = piece[half:]
        even, odd = right_dot(0, 2), right_dot(1, 3)
        total, difference = even + odd, even - odd
        for c, rows in enumerate(chunks):
            re = jnp.concatenate([total[rows, :half], difference[rows, :half]], 1)
            im = jnp.concatenate([total[rows, half:], difference[rows, half:]], 1)
            after(c, rows, re, im)

    rows, cols, corners = halos[0]
    wait_recv(rows[:4])
    start(corners)
    start(halos[1][0] + halos[1][1])
    wait_recv(rows[4:] + cols + corners)
    for copy in inner[0]:
        copy.wait()

    def enter(slot, nothing):
        def before(chunk, rows):
            return times(probe[0, rows], probe[1, rows], window(pad_one, slot, 0, chunk), window(pad_one, slot, 1, chunk))

        def between(rows, re, im):
            return times(wave[0, rows], wave[1, rows], re, im)

        def after(chunk, rows, re, im):
            carry[slot, 0, rows] = re
            carry[slot, 1, rows] = im

        there_and_back(before, between, after)
        return nothing

    lax.fori_loop(0, cap, enter, 0)

    rows, cols, corners = halos[1]
    wait_recv(rows[:4])
    start(corners)
    wait_recv(rows[4:] + cols + corners)
    for copy in inner[1]:
        copy.wait()

    def leave(slot, nothing):
        def before(chunk, rows):
            second[slot, 0, rows] = window(pad_two, slot, 0, chunk)
            second[slot, 1, rows] = window(pad_two, slot, 1, chunk)
            return times(carry[slot, 0, rows], carry[slot, 1, rows], second[slot, 0, rows], second[slot, 1, rows])

        def between(rows, re, im):
            misfit = re * re + im * im - measured[slot, rows]
            return misfit * re, misfit * im

        def after(chunk, rows, re, im):
            two_re, two_im = conj_times(carry[slot, 0, rows], carry[slot, 1, rows], re, im)
            put(place_two, slot, 0, chunk, two_re)
            put(place_two, slot, 1, chunk, two_im)
            back_re, back_im = conj_times(second[slot, 0, rows], second[slot, 1, rows], re, im)
            gcarry[slot, 0, rows] = back_re
            gcarry[slot, 1, rows] = back_im

        there_and_back(before, between, after)
        return nothing

    lax.fori_loop(0, cap, leave, 0)

    blocks = ext // half

    def gather_block(which, row_block, col_block):
        _, target, total, _, _ = slices[which]
        for comp in range(2):
            value = None
            for slot in range(cap):
                block, _ = column_of(slot)
                moved = col_block - block
                taken = jnp.where(jnp.logical_and(moved >= 0, moved <= 2), moved, 3)
                begin = jnp.clip(row_block * half - offsets[0, slot] + half, 0, 3 * half)
                piece = target[comp, slot, taken, pl.ds(begin, half), :]
                value = piece if value is None else value + piece
            rows = pl.ds(pl.multiple_of(row_block * half, half), half)
            cols = pl.ds(pl.multiple_of(col_block * half, half), half)
            total[comp, rows, cols] = value

    def gather_rows(which):
        def step(number, nothing):
            gather_block(which, (number // blocks) * (blocks - 1), number % blocks)
            return nothing

        lax.fori_loop(0, 2 * blocks, step, 0)

    def gather_cols(which):
        def step(number, nothing):
            gather_block(which, 1 + number // 2, (number % 2) * (blocks - 1))
            return nothing

        lax.fori_loop(0, 2 * (blocks - 2), step, 0)

    def gather_inner(which):
        def step(number, nothing):
            gather_block(which, 1 + number // (blocks - 2), 1 + number % (blocks - 2))
            return nothing

        lax.fori_loop(0, (blocks - 2) * (blocks - 2), step, 0)

    def send_sums(which):
        rows, cols, corners = folds[which]
        gather_rows(which)
        start(corners + rows[4:])
        gather_cols(which)
        start(cols)
        gather_inner(which)

    def pass_corners(which):
        rows, _, corners = folds[which]
        _, _, total, _, land_cols = slices[which]
        wait_recv(corners)
        for band, there in ((slice(0, low), has_up), (slice(high, ext), has_down)):
            for side, near, cell in ((0, has_left, slice(low, low + half)), (1, has_right, slice(high - half, high))):

                @pl.when(jnp.logical_and(there, near))
                def _():
                    for comp in range(2):
                        total[comp, band, cell] += land_cols[side, comp, band, :]

        start(rows[:4])

    def finish(which):
        rows, cols, corners = folds[which]
        _, _, total, land_rows, land_cols = slices[which]
        wait_recv(cols)
        for side, near, cell in ((0, has_left, slice(low, low + half)), (1, has_right, slice(high - half, high))):

            @pl.when(near)
            def _():
                for comp in range(2):
                    total[comp, low:high, cell] += land_cols[side, comp, low:high, :]

        wait_recv(rows)
        for side, near, cell in ((0, has_up, slice(low, low + half)), (1, has_down, slice(high - half, high))):

            @pl.when(near)
            def _():
                for comp in range(2):
                    total[comp, cell, low:high] += land_rows[side, comp]

        copy = pltpu.make_async_copy(
            total.at[:, low:high, low:high], out.at[2 * which : 2 * which + 2], local_sem.at[6 + which]
        )
        copy.start()
        return copy

    send_sums(1)

    def back(slot, nothing):
        def before(chunk, rows):
            return gcarry[slot, 0, rows], gcarry[slot, 1, rows]

        def between(rows, re, im):
            return conj_times(wave[0, rows], wave[1, rows], re, im)

        def after(chunk, rows, re, im):
            one_re, one_im = conj_times(probe[0, rows], probe[1, rows], re, im)
            put(place_one, slot, 0, chunk, one_re)
            put(place_one, slot, 1, chunk, one_im)

        there_and_back(before, between, after)

        @pl.when(slot == 1)
        def _():
            pass_corners(1)

        return nothing

    lax.fori_loop(0, cap, back, 0)

    send_sums(0)
    pass_corners(0)
    last = [finish(1)]
    last.append(finish(0))
    for exchange in halos + folds:
        for copies in exchange:
            wait_send(copies)
    for copy in last:
        copy.wait()


def shards(n_gx, n_gy, objects, probe_wave, prop_phase, intensity, offsets, counts):
    frame = intensity.shape[1]
    half = frame // 2
    cap = intensity.shape[0]
    tile = objects.shape[1]
    ext = tile + frame
    anywhere = pl.BlockSpec(memory_space=pl.ANY)
    field = pltpu.VMEM((cap, 2, frame, frame), F32)
    scratch = [
        *[pltpu.VMEM((2, ext // half, ext, half), F32)] * 2,
        *[pltpu.VMEM((2, cap, 4, 4 * half, half), F32)] * 2,
        *[pltpu.VMEM((2, ext, ext), F32)] * 2,
        *[pltpu.VMEM((2, 2, half, tile), F32)] * 2,
        *[pltpu.VMEM((2, 2, ext, half), F32)] * 2,
        field,
        field,
        field,
        pltpu.VMEM((2, frame, frame), F32),
        pltpu.VMEM((2, frame, frame), F32),
        pltpu.VMEM((cap, frame, frame), F32),
        pltpu.VMEM((cap, frame, frame), F32),
        pltpu.VMEM((6, half, half), F32),
        pltpu.VMEM((frame, frame), F32),
        pltpu.VMEM((4, 3 * frame, frame), BF16),
        pltpu.VMEM((4, frame, 3 * frame), BF16),
        pltpu.VMEM((2, frame, 2 * frame), BF16),
        pltpu.VMEM((2, 2 * frame, frame), BF16),
        pltpu.SMEM((2, cap), jnp.int32),
        pltpu.SMEM((1,), jnp.int32),
        pltpu.SemaphoreType.DMA((4 * COPIES,)),
        pltpu.SemaphoreType.DMA((4 * COPIES,)),
        pltpu.SemaphoreType.DMA((8,)),
        pltpu.SemaphoreType.DMA((2, tile // half)),
    ]
    return pl.pallas_call(
        functools.partial(kernel, n_gx, n_gy),
        out_shape=jax.ShapeDtypeStruct(objects.shape, F32),
        in_specs=[anywhere] * 7,
        out_specs=anywhere,
        scratch_shapes=scratch,
        compiler_params=pltpu.CompilerParams(
            collective_id=0, has_side_effects=True, vmem_limit_bytes=60 * 1024 * 1024
        ),
        name="ptychography",
    )(offsets.T, counts, objects, probe_wave, prop_phase, intensity, jnp.asarray(phase_tables(frame)))


def solution(mesh):
    return jax.shard_map(
        functools.partial(shards, mesh.shape["gx"], mesh.shape["gy"]),
        mesh=mesh,
        in_specs=(
            P(None, "gx", "gy"),
            P(),
            P(),
            P(("gx", "gy"), None, None),
            P(("gx", "gy"), None),
            P(("gx", "gy")),
        ),
        out_specs=P(None, "gx", "gy"),
        check_vma=False,
    )
```

```python
import functools

import jax
import jax.numpy as jnp
import numpy as np
from jax import lax
from jax.experimental import pallas as pl
from jax.experimental.pallas import tpu as pltpu
from jax.sharding import PartitionSpec as P

F32 = jnp.float32
BF16 = jnp.bfloat16
MESH = pl.DeviceIdType.MESH
CHUNK = 64
COPIES = 14
GROUP = 2
steps_end = object()


def phase_tables(frame_len):
    half = frame_len // 2
    n = np.arange(half)[:, None]
    k = np.arange(half)[None, :]
    factor = 1.0 / np.sqrt(frame_len)
    even = 2.0 * np.pi * (n * 2 * k % frame_len) / frame_len
    odd = 2.0 * np.pi * (n * (2 * k + 1) % frame_len) / frame_len
    parts = [np.cos(even), np.sin(even), np.cos(odd), np.sin(odd), np.cos(odd).T, np.sin(odd).T]
    return np.stack([part * factor for part in parts]).astype(np.float32)


def split(value):
    high = value.astype(BF16)
    return high, (value - high.astype(F32)).astype(BF16)


def dot(left, right):
    return jnp.dot(left, right, preferred_element_type=F32)


def times(left_re, left_im, right_re, right_im):
    return left_re * right_re - left_im * right_im, left_re * right_im + left_im * right_re


def conj_times(left_re, left_im, right_re, right_im):
    return left_re * right_re + left_im * right_im, left_re * right_im - left_im * right_re


def kernel(
    n_gx, n_gy, offsets_hbm, counts_hbm, objects, probe_hbm, phase_hbm, intensity_hbm, tables_hbm, out,
    pad_one, pad_two, place_one, place_two, top_one, top_two, side_one, side_two, rows_one, rows_two, cols_one, cols_two,
    carry, second, probe, wave, measured, tables, phase, weights_r, weights_l, rows_in, cols_in,
    offsets, counts, send_sem, recv_sem, local_sem, inner_sem,
):
    frame = probe.shape[1]
    half = frame // 2
    cap = intensity_hbm.shape[0]
    tile = objects.shape[1]
    ext = tile + frame
    low, high = half, half + tile
    gx, gy = lax.axis_index("gx"), lax.axis_index("gy")
    has_up, has_down = gx > 0, gx < n_gx - 1
    has_left, has_right = gy > 0, gy < n_gy - 1
    up, down, left, right = (gx - 1, gy), (gx + 1, gy), (gx, gy - 1), (gx, gy + 1)
    slices = (
        (pad_one, place_one, top_one, side_one, rows_one, cols_one),
        (pad_two, place_two, top_two, side_two, rows_two, cols_two),
    )

    local = [
        pltpu.make_async_copy(tables_hbm, tables, local_sem.at[0]),
        pltpu.make_async_copy(phase_hbm, phase, local_sem.at[1]),
        pltpu.make_async_copy(intensity_hbm, measured, local_sem.at[2]),
        pltpu.make_async_copy(probe_hbm, probe, local_sem.at[3]),
        pltpu.make_async_copy(offsets_hbm, offsets, local_sem.at[4]),
        pltpu.make_async_copy(counts_hbm, counts, local_sem.at[5]),
    ]
    inner = [
        [
            pltpu.make_async_copy(
                objects.at[2 * which : 2 * which + 2, :, block * half : (block + 1) * half],
                pad.at[:, block + 1, low:high],
                inner_sem.at[which, block],
            )
            for block in range(tile // half)
        ]
        for which, pad in enumerate((pad_one, pad_two))
    ]
    local += inner[0] + inner[1]
    for copy in local:
        copy.start()

    barrier = pltpu.get_barrier_semaphore()
    sides = ((has_up, up), (has_down, down), (has_left, left), (has_right, right))
    for there, device in sides:

        @pl.when(there)
        def _():
            pl.semaphore_signal(barrier, inc=1, device_id=device, device_id_type=MESH)

    pl.semaphore_wait(barrier, sum(there.astype(jnp.int32) for there, _ in sides))

    def remote(number, source, target, device, sends, receives):
        copy = pltpu.make_async_remote_copy(
            src_ref=source, dst_ref=target, send_sem=send_sem.at[number], recv_sem=recv_sem.at[number],
            device_id=device, device_id_type=MESH,
        )
        return sends, receives, copy

    def start(copies):
        for sends, _, copy in copies:
            pl.when(sends)(copy.start)

    def wait_recv(copies):
        for _, receives, copy in copies:
            pl.when(receives)(copy.wait_recv)

    def wait_send(copies):
        for sends, _, copy in copies:
            pl.when(sends)(copy.wait_send)

    edge_pieces = (slice(0, half), slice(tile - half, tile))
    middle = slice(half, tile - half)

    def shift_by(piece, distance):
        return slice(piece.start + distance, piece.stop + distance)

    def halo(which):
        pad = slices[which][0]
        cells = objects.at[2 * which : 2 * which + 2]
        base = which * COPIES
        rows = []
        blocks = tile // half
        for block in (0, blocks - 1, *range(1, blocks - 1)):
            piece = slice(block * half, (block + 1) * half)
            rows.append(
                remote(base + len(rows), cells.at[:, 0:half, piece], pad.at[:, block + 1, high:ext], up, has_up, has_down)
            )
            rows.append(
                remote(base + len(rows), cells.at[:, tile - half : tile, piece], pad.at[:, block + 1, 0:low], down, has_down, has_up)
            )
        cols = [
            remote(base + 8, cells.at[:, :, 0:half], pad.at[:, blocks + 1, low:high], left, has_left, has_right),
            remote(base + 9, cells.at[:, :, tile - half : tile], pad.at[:, 0, low:high], right, has_right, has_left),
        ]
        corners = []
        for band, there in ((slice(0, low), has_up), (slice(high, ext), has_down)):
            to_left, to_right = jnp.logical_and(there, has_left), jnp.logical_and(there, has_right)
            corners.append(
                remote(base + 10 + len(corners), pad.at[:, 1, band], pad.at[:, blocks + 1, band], left, to_left, to_right)
            )
            corners.append(
                remote(base + 10 + len(corners), pad.at[:, blocks, band], pad.at[:, 0, band], right, to_right, to_left)
            )
        return rows, cols, corners

    def fold(which):
        _, _, top, side, land_rows, land_cols = slices[which]
        base = (2 + which) * COPIES
        rows = []
        for piece in (*edge_pieces, middle):
            moved = shift_by(piece, half)
            rows.append(
                remote(base + len(rows), top.at[:, 0, :, moved], land_rows.at[1, :, :, piece], up, has_up, has_down)
            )
            rows.append(
                remote(base + len(rows), top.at[:, 1, :, moved], land_rows.at[0, :, :, piece], down, has_down, has_up)
            )
        cols = [
            remote(base + 6, side.at[:, 0], land_cols.at[1, :, low:high], left, has_left, has_right),
            remote(base + 7, side.at[:, 1], land_cols.at[0, :, low:high], right, has_right, has_left),
        ]
        corners = []
        for edge, band, there in ((0, slice(0, low), has_up), (1, slice(high, ext), has_down)):
            to_left, to_right = jnp.logical_and(there, has_left), jnp.logical_and(there, has_right)
            corners.append(
                remote(base + 8 + len(corners), top.at[:, edge, :, 0:low], land_cols.at[1, :, band], left, to_left, to_right)
            )
            corners.append(
                remote(base + 8 + len(corners), top.at[:, edge, :, high:ext], land_cols.at[0, :, band], right, to_right, to_left)
            )
        return rows, cols, corners

    halos = [halo(0), halo(1)]
    folds = [fold(0), fold(1)]

    start(halos[0][0] + halos[0][1])

    for pad in (pad_one, pad_two):

        @pl.when(jnp.logical_not(has_up))
        def _():
            pad[:, :, 0:low] = jnp.zeros((2, ext // half, low, half), F32)

        @pl.when(jnp.logical_not(has_down))
        def _():
            pad[:, :, high:ext] = jnp.zeros((2, ext // half, low, half), F32)

        @pl.when(jnp.logical_not(has_left))
        def _():
            pad[:, 0] = jnp.zeros((2, ext, half), F32)

        @pl.when(jnp.logical_not(has_right))
        def _():
            pad[:, ext // half - 1] = jnp.zeros((2, ext, half), F32)

    local[0].wait()
    cos_e, sin_e, cos_o, sin_o, cos_t, sin_t = (tables[i] for i in range(6))

    def real_form(cosine, sine):
        return jnp.concatenate([jnp.concatenate([cosine, -sine], 1), jnp.concatenate([sine, cosine], 1)], 0)

    forms = (real_form(cos_e, sin_e), real_form(cos_o, sin_o), real_form(cos_e, -sin_e), real_form(cos_t, -sin_t))
    for number, form in enumerate(forms):
        top, rest = split(form)
        for part, value in enumerate((top, top, rest)):
            weights_r[number, part * frame : (part + 1) * frame, :] = value
            weights_l[number, :, part * frame : (part + 1) * frame] = value

    place = lax.broadcasted_iota(jnp.int32, (frame, frame), 0)
    other = lax.broadcasted_iota(jnp.int32, (frame, frame), 1)

    def picked(i):
        return jnp.where(i < half, 2 * i, 2 * (i - half) + 1)

    pick_rows = jnp.where(other == picked(place), 1.0, 0.0).astype(BF16)
    pick_cols = jnp.where(place == picked(other), 1.0, 0.0).astype(BF16)

    def sorted_frequencies(value):
        for axis in (0, 1):
            top, rest = split(value)
            middle_part, last = split(value - top.astype(F32))
            del rest
            parts = (top, middle_part, last)
            if axis == 0:
                value = sum(dot(pick_rows, part) for part in parts[::-1])
            else:
                value = sum(dot(part, pick_cols) for part in parts[::-1])
        return value

    local[1].wait()
    angle = sorted_frequencies(phase[...])
    wave[0] = jnp.cos(angle)
    wave[1] = jnp.sin(angle)
    local[2].wait()

    def sort_slot(slot, nothing):
        measured[slot] = sorted_frequencies(measured[slot])
        return nothing

    lax.fori_loop(0, cap, sort_slot, 0)

    rows, cols, corners = halos[0]
    wait_recv(rows[:4])
    start(corners)
    start(halos[1][0] + halos[1][1])

    def clear_place(slot, nothing):
        for target in (place_one, place_two):
            for comp in range(2):
                target[comp, slot, 3] = jnp.zeros((4 * half, half), F32)
                for block in range(3):
                    target[comp, slot, block, 0:half] = jnp.zeros((half, half), F32)
                    target[comp, slot, block, 3 * half : 4 * half] = jnp.zeros((half, half), F32)
        return nothing

    lax.fori_loop(0, cap, clear_place, 0)
    local[3].wait()
    local[4].wait()
    local[5].wait()

    lane = lax.broadcasted_iota(jnp.int32, (CHUNK, half), 1)

    def column_of(slot):
        column = offsets[1, slot]
        block = jnp.minimum(column // half, tile // half - 1)
        return block, column - block * half

    def window(pad, slot, comp, chunk):
        row = offsets[0, slot]
        block, shift = column_of(slot)
        rows = pl.ds(row + chunk * CHUNK, CHUNK)
        back = jnp.where(jnp.logical_or(shift == 0, shift == half), 0, half - shift)
        turned = [pltpu.roll(pad[comp, block + i, rows, :], back, 1) for i in range(3)]
        kept = lane < half - shift
        return jnp.concatenate([jnp.where(kept, turned[i], turned[i + 1]) for i in range(2)], 1)

    def put(target, slot, comp, chunk, value):
        _, shift = column_of(slot)
        turn = jnp.where(shift == half, 0, shift)
        value = jnp.where(slot < counts[0], value, jnp.zeros_like(value))
        first = pltpu.roll(value[:, :half], turn, 1)
        last = pltpu.roll(value[:, half:], turn, 1)
        inside = lane >= shift
        nothing = jnp.zeros_like(first)
        rows = slice(half + chunk * CHUNK, half + (chunk + 1) * CHUNK)
        target[comp, slot, 0, rows] = jnp.where(inside, first, nothing)
        target[comp, slot, 1, rows] = jnp.where(inside, last, first)
        target[comp, slot, 2, rows] = jnp.where(inside, nothing, last)

    def right_dot(lane_of, j, number):
        value = rows_in[lane_of, j]
        return dot(jnp.concatenate([value, value[:, :frame]], 1), weights_r[number])

    def left_dot(lane_of, i, number):
        value = cols_in[lane_of, i]
        return dot(weights_l[number], jnp.concatenate([value, value[:frame]], 0))

    def there_and_back(which, before, between, after):
        chunks = [slice(c * CHUNK, (c + 1) * CHUNK) for c in range(frame // CHUNK)]
        for c, rows in enumerate(chunks):
            re, im = before(c, rows)
            for j in range(2):
                if j == 0:
                    mixed = jnp.concatenate([re[:, :half] + re[:, half:], im[:, :half] + im[:, half:]], 1)
                else:
                    mixed = jnp.concatenate([re[:, :half] - re[:, half:], im[:, :half] - im[:, half:]], 1)
                top, rest = split(mixed)
                rows_in[which, j, rows, 0:frame] = top
                rows_in[which, j, rows, frame : 2 * frame] = rest
        yield
        for j in range(2):
            value = right_dot(which, j, j)
            cols = slice(j * half, (j + 1) * half)
            for i in range(2):
                mixed = value[:half] + value[half:] if i == 0 else value[:half] - value[half:]
                for part, piece in enumerate(split(mixed)):
                    cols_in[which, i, part * frame : part * frame + half, cols] = piece[:, :half]
                    cols_in[which, i, part * frame + half : (part + 1) * frame, cols] = piece[:, half:]
        yield
        for i in range(2):
            value = left_dot(which, i, 2 + i)
            re, im = between(slice(i * half, (i + 1) * half), value[:half], value[half:])
            for position, field in enumerate((re, im)):
                for part, piece in enumerate(split(field)):
                    begin = part * frame + position * half
                    cols_in[which, i, begin : begin + half, :] = piece
        yield
        even, odd = left_dot(which, 0, 0), left_dot(which, 1, 1)
        for i in range(2):
            mixed = even + odd if i == 0 else even - odd
            rows = slice(i * half, (i + 1) * half)
            for j in range(2):
                for part, piece in enumerate(split(mixed[:, j * half : (j + 1) * half])):
                    begin = part * frame
                    rows_in[which, j, rows, begin : begin + half] = piece[:half]
                    rows_in[which, j, rows, begin + half : begin + frame] = piece[half:]
        yield
        even, odd = right_dot(which, 0, 2), right_dot(which, 1, 3)
        total, difference = even + odd, even - odd
        for c, rows in enumerate(chunks):
            re = jnp.concatenate([total[rows, :half], difference[rows, :half]], 1)
            im = jnp.concatenate([total[rows, half:], difference[rows, half:]], 1)
            after(c, rows, re, im)

    def frames(steps_of, then=None):
        def group(number, nothing):
            waiting = [steps_of(which, number * GROUP + which) for which in range(GROUP)]
            running = []
            while waiting or running:
                if waiting:
                    running.append(waiting.pop(0))
                running = [steps for steps in running if next(steps, steps_end) is not steps_end]
            if then is not None:
                then(number)
            return nothing

        lax.fori_loop(0, cap // GROUP, group, 0)

    wait_recv(rows[4:] + cols + corners)
    for copy in inner[0]:
        copy.wait()

    def enter(which, slot):
        def before(chunk, rows):
            return times(probe[0, rows], probe[1, rows], window(pad_one, slot, 0, chunk), window(pad_one, slot, 1, chunk))

        def between(rows, re, im):
            return times(wave[0, rows], wave[1, rows], re, im)

        def after(chunk, rows, re, im):
            carry[slot, 0, rows] = re
            carry[slot, 1, rows] = im

        return there_and_back(which, before, between, after)

    frames(enter)

    rows, cols, corners = halos[1]
    wait_recv(rows[:4])
    start(corners)
    wait_recv(rows[4:] + cols + corners)
    for copy in inner[1]:
        copy.wait()

    def leave(which, slot):
        def before(chunk, rows):
            second[slot, 0, rows] = window(pad_two, slot, 0, chunk)
            second[slot, 1, rows] = window(pad_two, slot, 1, chunk)
            return times(carry[slot, 0, rows], carry[slot, 1, rows], second[slot, 0, rows], second[slot, 1, rows])

        def between(rows, re, im):
            misfit = re * re + im * im - measured[slot, rows]
            return misfit * re, misfit * im

        def after(chunk, rows, re, im):
            two_re, two_im = conj_times(carry[slot, 0, rows], carry[slot, 1, rows], re, im)
            put(place_two, slot, 0, chunk, two_re)
            put(place_two, slot, 1, chunk, two_im)
            back_re, back_im = conj_times(second[slot, 0, rows], second[slot, 1, rows], re, im)
            second[slot, 0, rows] = back_re
            second[slot, 1, rows] = back_im

        return there_and_back(which, before, between, after)

    frames(leave)

    blocks = ext // half
    last = blocks - 1

    def gathered(which, comp, row_block, col_block):
        target = slices[which][1]
        value = None
        for slot in range(cap):
            block, _ = column_of(slot)
            moved = col_block - block
            taken = jnp.where(jnp.logical_and(moved >= 0, moved <= 2), moved, 3)
            begin = jnp.clip(row_block * half - offsets[0, slot] + half, 0, 3 * half)
            piece = target[comp, slot, taken, pl.ds(begin, half), :]
            value = piece if value is None else value + piece
        return value

    def block_at(number):
        return pl.ds(pl.multiple_of(number * half, half), half)

    def gather_top(which, first_col, step_col):
        top = slices[which][2]

        def step(number, nothing):
            edge, col_block = number // 2, first_col + number % 2 * step_col
            for comp in range(2):
                top[comp, edge, :, block_at(col_block)] = gathered(which, comp, edge * last, col_block)
            return nothing

        lax.fori_loop(0, 4, step, 0)

    def gather_sides(which):
        side = slices[which][3]

        def step(number, nothing):
            near, row_block = number % 2, number // 2
            for comp in range(2):
                side[comp, near, block_at(row_block), :] = gathered(which, comp, row_block + 1, near * last)
            return nothing

        lax.fori_loop(0, 2 * (blocks - 2), step, 0)

    def gather_inner(which):
        def step(number, nothing):
            row_block, col_block = number // (blocks - 2), number % (blocks - 2)
            for comp in range(2):
                out[2 * which + comp, block_at(row_block), block_at(col_block)] = gathered(
                    which, comp, row_block + 1, col_block + 1
                )
            return nothing

        lax.fori_loop(0, (blocks - 2) * (blocks - 2), step, 0)

    def send_sums(which):
        rows, cols, corners = folds[which]
        gather_top(which, 0, last)
        start(corners)
        gather_top(which, 2, 1)
        start(rows[4:])
        gather_top(which, 1, last - 2)
        gather_sides(which)
        start(cols)
        gather_inner(which)

    def pass_corners(which):
        rows, _, corners = folds[which]
        _, _, top, _, _, land_cols = slices[which]
        wait_recv(corners)
        for edge, band, there in ((0, slice(0, low), has_up), (1, slice(high, ext), has_down)):
            for side, near, cell in ((0, has_left, slice(low, low + half)), (1, has_right, slice(high - half, high))):

                @pl.when(jnp.logical_and(there, near))
                def _():
                    for comp in range(2):
                        top[comp, edge, :, cell] += land_cols[side, comp, band, :]

        start(rows[:4])

    def finish(which):
        rows, cols, _ = folds[which]
        _, _, _, _, land_rows, land_cols = slices[which]
        wait_recv(cols)
        for side, near, cell in ((0, has_left, edge_pieces[0]), (1, has_right, edge_pieces[1])):

            @pl.when(near)
            def _():
                for comp in range(2):
                    out[2 * which + comp, :, cell] += land_cols[side, comp, low:high, :]

        for arrived, pieces in ((rows[4:], (middle,)), (rows[:4], edge_pieces)):
            wait_recv(arrived)
            for side, near, cell in ((0, has_up, edge_pieces[0]), (1, has_down, edge_pieces[1])):

                @pl.when(near)
                def _():
                    for comp in range(2):
                        for piece in pieces:
                            out[2 * which + comp, cell, piece] += land_rows[side, comp, :, piece]

    send_sums(1)

    def back(which, slot):
        def before(chunk, rows):
            return second[slot, 0, rows], second[slot, 1, rows]

        def between(rows, re, im):
            return conj_times(wave[0, rows], wave[1, rows], re, im)

        def after(chunk, rows, re, im):
            one_re, one_im = conj_times(probe[0, rows], probe[1, rows], re, im)
            put(place_one, slot, 0, chunk, one_re)
            put(place_one, slot, 1, chunk, one_im)

        return there_and_back(which, before, between, after)

    def between_groups(number):
        @pl.when(number == 0)
        def _():
            pass_corners(1)

    frames(back, between_groups)

    send_sums(0)
    pass_corners(0)
    finish(1)
    finish(0)
    for exchange in halos + folds:
        for copies in exchange:
            wait_send(copies)


def shards(n_gx, n_gy, objects, probe_wave, prop_phase, intensity, offsets, counts):
    frame = intensity.shape[1]
    half = frame // 2
    cap = intensity.shape[0]
    tile = objects.shape[1]
    ext = tile + frame
    anywhere = pl.BlockSpec(memory_space=pl.ANY)
    field = pltpu.VMEM((cap, 2, frame, frame), F32)
    scratch = [
        *[pltpu.VMEM((2, ext // half, ext, half), F32)] * 2,
        *[pltpu.VMEM((2, cap, 4, 4 * half, half), F32)] * 2,
        *[pltpu.VMEM((2, 2, half, ext), F32)] * 2,
        *[pltpu.VMEM((2, 2, tile, half), F32)] * 2,
        *[pltpu.VMEM((2, 2, half, tile), F32)] * 2,
        *[pltpu.VMEM((2, 2, ext, half), F32)] * 2,
        field,
        field,
        pltpu.VMEM((2, frame, frame), F32),
        pltpu.VMEM((2, frame, frame), F32),
        pltpu.VMEM((cap, frame, frame), F32),
        pltpu.VMEM((6, half, half), F32),
        pltpu.VMEM((frame, frame), F32),
        pltpu.VMEM((4, 3 * frame, frame), BF16),
        pltpu.VMEM((4, frame, 3 * frame), BF16),
        pltpu.VMEM((GROUP, 2, frame, 2 * frame), BF16),
        pltpu.VMEM((GROUP, 2, 2 * frame, frame), BF16),
        pltpu.SMEM((2, cap), jnp.int32),
        pltpu.SMEM((1,), jnp.int32),
        pltpu.SemaphoreType.DMA((4 * COPIES,)),
        pltpu.SemaphoreType.DMA((4 * COPIES,)),
        pltpu.SemaphoreType.DMA((8,)),
        pltpu.SemaphoreType.DMA((2, tile // half)),
    ]
    return pl.pallas_call(
        functools.partial(kernel, n_gx, n_gy),
        out_shape=pltpu.VMEM(objects.shape, F32),
        in_specs=[anywhere] * 7,
        out_specs=pl.BlockSpec(memory_space=pltpu.VMEM),
        scratch_shapes=scratch,
        compiler_params=pltpu.CompilerParams(
            collective_id=0, has_side_effects=True, vmem_limit_bytes=58 * 1024 * 1024
        ),
        name="ptychography",
    )(offsets.T, counts, objects, probe_wave, prop_phase, intensity, jnp.asarray(phase_tables(frame)))


def solution(mesh):
    return jax.shard_map(
        functools.partial(shards, mesh.shape["gx"], mesh.shape["gy"]),
        mesh=mesh,
        in_specs=(
            P(None, "gx", "gy"),
            P(),
            P(),
            P(("gx", "gy"), None, None),
            P(("gx", "gy"), None),
            P(("gx", "gy")),
        ),
        out_specs=P(None, "gx", "gy"),
        check_vma=False,
    )
```

```python
import functools

import jax
import jax.numpy as jnp
import numpy as np
from jax import lax
from jax.experimental import pallas as pl
from jax.experimental.pallas import tpu as pltpu
from jax.sharding import PartitionSpec as P

F32 = jnp.float32
BF16 = jnp.bfloat16
MESH = pl.DeviceIdType.MESH
CHUNK = 64
COPIES = 14
GROUP = 2
steps_end = object()


def phase_tables(frame_len):
    half = frame_len // 2
    n = np.arange(half)[:, None]
    k = np.arange(half)[None, :]
    factor = 1.0 / np.sqrt(frame_len)
    even = 2.0 * np.pi * (n * 2 * k % frame_len) / frame_len
    odd = 2.0 * np.pi * (n * (2 * k + 1) % frame_len) / frame_len
    parts = [np.cos(even), np.sin(even), np.cos(odd), np.sin(odd), np.cos(odd).T, np.sin(odd).T]
    return np.stack([part * factor for part in parts]).astype(np.float32)


def split(value):
    high = value.astype(BF16)
    return high, (value - high.astype(F32)).astype(BF16)


def dot(left, right):
    return jnp.dot(left, right, preferred_element_type=F32)


def times(left_re, left_im, right_re, right_im):
    return left_re * right_re - left_im * right_im, left_re * right_im + left_im * right_re


def conj_times(left_re, left_im, right_re, right_im):
    return left_re * right_re + left_im * right_im, left_re * right_im - left_im * right_re


def kernel(
    n_gx, n_gy, offsets_hbm, counts_hbm, objects, probe_hbm, phase_hbm, intensity_hbm, tables_hbm, out,
    pad_one, pad_two, place_one, place_two, top_one, top_two, side_one, side_two, rows_one, rows_two, cols_one, cols_two,
    carry, second, gexit, probe, wave, measured, tables, phase, weights_r, weights_l, rows_in, cols_in,
    offsets, counts, send_sem, recv_sem, local_sem, inner_sem,
):
    frame = probe.shape[1]
    half = frame // 2
    cap = intensity_hbm.shape[0]
    tile = objects.shape[1]
    ext = tile + frame
    low, high = half, half + tile
    gx, gy = lax.axis_index("gx"), lax.axis_index("gy")
    has_up, has_down = gx > 0, gx < n_gx - 1
    has_left, has_right = gy > 0, gy < n_gy - 1
    up, down, left, right = (gx - 1, gy), (gx + 1, gy), (gx, gy - 1), (gx, gy + 1)
    slices = (
        (pad_one, place_one, top_one, side_one, rows_one, cols_one),
        (pad_two, place_two, top_two, side_two, rows_two, cols_two),
    )

    local = [
        pltpu.make_async_copy(tables_hbm, tables, local_sem.at[0]),
        pltpu.make_async_copy(phase_hbm, phase, local_sem.at[1]),
        pltpu.make_async_copy(intensity_hbm, measured, local_sem.at[2]),
        pltpu.make_async_copy(probe_hbm, probe, local_sem.at[3]),
        pltpu.make_async_copy(offsets_hbm, offsets, local_sem.at[4]),
        pltpu.make_async_copy(counts_hbm, counts, local_sem.at[5]),
    ]
    inner = [
        [
            pltpu.make_async_copy(
                objects.at[2 * which : 2 * which + 2, :, block * half : (block + 1) * half],
                pad.at[:, block + 1, low:high],
                inner_sem.at[which, block],
            )
            for block in range(tile // half)
        ]
        for which, pad in enumerate((pad_one, pad_two))
    ]
    local += inner[0] + inner[1]
    for copy in local:
        copy.start()

    barrier = pltpu.get_barrier_semaphore()
    sides = ((has_up, up), (has_down, down), (has_left, left), (has_right, right))
    for there, device in sides:

        @pl.when(there)
        def _():
            pl.semaphore_signal(barrier, inc=1, device_id=device, device_id_type=MESH)

    pl.semaphore_wait(barrier, sum(there.astype(jnp.int32) for there, _ in sides))

    def remote(number, source, target, device, sends, receives):
        copy = pltpu.make_async_remote_copy(
            src_ref=source, dst_ref=target, send_sem=send_sem.at[number], recv_sem=recv_sem.at[number],
            device_id=device, device_id_type=MESH,
        )
        return sends, receives, copy

    def start(copies):
        for sends, _, copy in copies:
            pl.when(sends)(copy.start)

    def wait_recv(copies):
        for _, receives, copy in copies:
            pl.when(receives)(copy.wait_recv)

    def wait_send(copies):
        for sends, _, copy in copies:
            pl.when(sends)(copy.wait_send)

    edge_pieces = (slice(0, half), slice(tile - half, tile))
    middle = slice(half, tile - half)

    def shift_by(piece, distance):
        return slice(piece.start + distance, piece.stop + distance)

    def halo(which):
        pad = slices[which][0]
        cells = objects.at[2 * which : 2 * which + 2]
        base = which * COPIES
        rows = []
        blocks = tile // half
        for block in (0, blocks - 1, *range(1, blocks - 1)):
            piece = slice(block * half, (block + 1) * half)
            rows.append(
                remote(base + len(rows), cells.at[:, 0:half, piece], pad.at[:, block + 1, high:ext], up, has_up, has_down)
            )
            rows.append(
                remote(base + len(rows), cells.at[:, tile - half : tile, piece], pad.at[:, block + 1, 0:low], down, has_down, has_up)
            )
        cols = [
            remote(base + 8, cells.at[:, :, 0:half], pad.at[:, blocks + 1, low:high], left, has_left, has_right),
            remote(base + 9, cells.at[:, :, tile - half : tile], pad.at[:, 0, low:high], right, has_right, has_left),
        ]
        corners = []
        for band, there in ((slice(0, low), has_up), (slice(high, ext), has_down)):
            to_left, to_right = jnp.logical_and(there, has_left), jnp.logical_and(there, has_right)
            corners.append(
                remote(base + 10 + len(corners), pad.at[:, 1, band], pad.at[:, blocks + 1, band], left, to_left, to_right)
            )
            corners.append(
                remote(base + 10 + len(corners), pad.at[:, blocks, band], pad.at[:, 0, band], right, to_right, to_left)
            )
        return rows, cols, corners

    def fold(which):
        _, _, top, side, land_rows, land_cols = slices[which]
        base = (2 + which) * COPIES
        rows = []
        for piece in (*edge_pieces, middle):
            moved = shift_by(piece, half)
            rows.append(
                remote(base + len(rows), top.at[:, 0, :, moved], land_rows.at[1, :, :, piece], up, has_up, has_down)
            )
            rows.append(
                remote(base + len(rows), top.at[:, 1, :, moved], land_rows.at[0, :, :, piece], down, has_down, has_up)
            )
        cols = [
            remote(base + 6, side.at[:, 0], land_cols.at[1, :, low:high], left, has_left, has_right),
            remote(base + 7, side.at[:, 1], land_cols.at[0, :, low:high], right, has_right, has_left),
        ]
        corners = []
        for edge, band, there in ((0, slice(0, low), has_up), (1, slice(high, ext), has_down)):
            to_left, to_right = jnp.logical_and(there, has_left), jnp.logical_and(there, has_right)
            corners.append(
                remote(base + 8 + len(corners), top.at[:, edge, :, 0:low], land_cols.at[1, :, band], left, to_left, to_right)
            )
            corners.append(
                remote(base + 8 + len(corners), top.at[:, edge, :, high:ext], land_cols.at[0, :, band], right, to_right, to_left)
            )
        return rows, cols, corners

    halos = [halo(0), halo(1)]
    folds = [fold(0), fold(1)]

    (rows_a, cols_a, corners_a), (rows_b, cols_b, corners_b) = halos
    start(rows_a[:4] + rows_b[:4] + cols_a)

    for pad in (pad_one, pad_two):

        @pl.when(jnp.logical_not(has_up))
        def _():
            pad[:, :, 0:low] = jnp.zeros((2, ext // half, low, half), F32)

        @pl.when(jnp.logical_not(has_down))
        def _():
            pad[:, :, high:ext] = jnp.zeros((2, ext // half, low, half), F32)

        @pl.when(jnp.logical_not(has_left))
        def _():
            pad[:, 0] = jnp.zeros((2, ext, half), F32)

        @pl.when(jnp.logical_not(has_right))
        def _():
            pad[:, ext // half - 1] = jnp.zeros((2, ext, half), F32)

    local[0].wait()
    cos_e, sin_e, cos_o, sin_o, cos_t, sin_t = (tables[i] for i in range(6))

    def real_form(cosine, sine):
        return jnp.concatenate([jnp.concatenate([cosine, -sine], 1), jnp.concatenate([sine, cosine], 1)], 0)

    forms = (real_form(cos_e, sin_e), real_form(cos_o, sin_o), real_form(cos_e, -sin_e), real_form(cos_t, -sin_t))
    for number, form in enumerate(forms):
        top, rest = split(form)
        for part, value in enumerate((top, top, rest)):
            weights_r[number, part * frame : (part + 1) * frame, :] = value
            weights_l[number, :, part * frame : (part + 1) * frame] = value

    place = lax.broadcasted_iota(jnp.int32, (frame, frame), 0)
    other = lax.broadcasted_iota(jnp.int32, (frame, frame), 1)

    def picked(i):
        return jnp.where(i < half, 2 * i, 2 * (i - half) + 1)

    pick_rows = jnp.where(other == picked(place), 1.0, 0.0).astype(BF16)
    pick_cols = jnp.where(place == picked(other), 1.0, 0.0).astype(BF16)

    def sorted_frequencies(value):
        for axis in (0, 1):
            top, rest = split(value)
            middle_part, last = split(value - top.astype(F32))
            del rest
            parts = (top, middle_part, last)
            if axis == 0:
                value = sum(dot(pick_rows, part) for part in parts[::-1])
            else:
                value = sum(dot(part, pick_cols) for part in parts[::-1])
        return value

    local[1].wait()
    angle = sorted_frequencies(phase[...])
    wave[0] = jnp.cos(angle)
    wave[1] = jnp.sin(angle)
    wait_send(rows_a[:4])
    start(rows_a[4:] + cols_b)
    local[2].wait()

    def sort_slot(slot, nothing):
        measured[slot] = sorted_frequencies(measured[slot])
        return nothing

    lax.fori_loop(0, cap, sort_slot, 0)

    wait_recv(rows_a[:4])
    start(corners_a)

    def clear_place(slot, nothing):
        for target in (place_one, place_two):
            for comp in range(2):
                target[comp, slot, 3] = jnp.zeros((4 * half, half), F32)
                for block in range(3):
                    target[comp, slot, block, 0:half] = jnp.zeros((half, half), F32)
                    target[comp, slot, block, 3 * half : 4 * half] = jnp.zeros((half, half), F32)
        return nothing

    lax.fori_loop(0, cap, clear_place, 0)
    local[3].wait()
    local[4].wait()
    local[5].wait()

    lane = lax.broadcasted_iota(jnp.int32, (CHUNK, half), 1)

    def column_of(slot):
        column = offsets[1, slot]
        block = jnp.minimum(column // half, tile // half - 1)
        return block, column - block * half

    def window(pad, slot, comp, chunk):
        row = offsets[0, slot]
        block, shift = column_of(slot)
        rows = pl.ds(row + chunk * CHUNK, CHUNK)
        back = jnp.where(jnp.logical_or(shift == 0, shift == half), 0, half - shift)
        turned = [pltpu.roll(pad[comp, block + i, rows, :], back, 1) for i in range(3)]
        kept = lane < half - shift
        return jnp.concatenate([jnp.where(kept, turned[i], turned[i + 1]) for i in range(2)], 1)

    def put(target, slot, comp, chunk, value):
        _, shift = column_of(slot)
        turn = jnp.where(shift == half, 0, shift)
        value = jnp.where(slot < counts[0], value, jnp.zeros_like(value))
        first = pltpu.roll(value[:, :half], turn, 1)
        last = pltpu.roll(value[:, half:], turn, 1)
        inside = lane >= shift
        nothing = jnp.zeros_like(first)
        rows = slice(half + chunk * CHUNK, half + (chunk + 1) * CHUNK)
        target[comp, slot, 0, rows] = jnp.where(inside, first, nothing)
        target[comp, slot, 1, rows] = jnp.where(inside, last, first)
        target[comp, slot, 2, rows] = jnp.where(inside, nothing, last)

    def right_dot(lane_of, j, number):
        value = rows_in[lane_of, j]
        return dot(jnp.concatenate([value, value[:, :frame]], 1), weights_r[number])

    def left_dot(lane_of, i, number):
        value = cols_in[lane_of, i]
        return dot(weights_l[number], jnp.concatenate([value, value[:frame]], 0))

    def there_and_back(which, before, between, after):
        chunks = [slice(c * CHUNK, (c + 1) * CHUNK) for c in range(frame // CHUNK)]
        for c, rows in enumerate(chunks):
            re, im = before(c, rows)
            for j in range(2):
                if j == 0:
                    mixed = jnp.concatenate([re[:, :half] + re[:, half:], im[:, :half] + im[:, half:]], 1)
                else:
                    mixed = jnp.concatenate([re[:, :half] - re[:, half:], im[:, :half] - im[:, half:]], 1)
                top, rest = split(mixed)
                rows_in[which, j, rows, 0:frame] = top
                rows_in[which, j, rows, frame : 2 * frame] = rest
        yield
        for j in range(2):
            value = right_dot(which, j, j)
            cols = slice(j * half, (j + 1) * half)
            for i in range(2):
                mixed = value[:half] + value[half:] if i == 0 else value[:half] - value[half:]
                for part, piece in enumerate(split(mixed)):
                    cols_in[which, i, part * frame : part * frame + half, cols] = piece[:, :half]
                    cols_in[which, i, part * frame + half : (part + 1) * frame, cols] = piece[:, half:]
        yield
        for i in range(2):
            value = left_dot(which, i, 2 + i)
            re, im = between(slice(i * half, (i + 1) * half), value[:half], value[half:])
            for position, field in enumerate((re, im)):
                for part, piece in enumerate(split(field)):
                    begin = part * frame + position * half
                    cols_in[which, i, begin : begin + half, :] = piece
        yield
        even, odd = left_dot(which, 0, 0), left_dot(which, 1, 1)
        for i in range(2):
            mixed = even + odd if i == 0 else even - odd
            rows = slice(i * half, (i + 1) * half)
            for j in range(2):
                for part, piece in enumerate(split(mixed[:, j * half : (j + 1) * half])):
                    begin = part * frame
                    rows_in[which, j, rows, begin : begin + half] = piece[:half]
                    rows_in[which, j, rows, begin + half : begin + frame] = piece[half:]
        yield
        even, odd = right_dot(which, 0, 2), right_dot(which, 1, 3)
        total, difference = even + odd, even - odd
        for c, rows in enumerate(chunks):
            re = jnp.concatenate([total[rows, :half], difference[rows, :half]], 1)
            im = jnp.concatenate([total[rows, half:], difference[rows, half:]], 1)
            after(c, rows, re, im)

    def frames(steps_of, then=None):
        def group(number, nothing):
            running = [steps_of(which, number * GROUP + which) for which in range(GROUP)]
            while running:
                running = [steps for steps in running if next(steps, steps_end) is not steps_end]
            if then is not None:
                then(number)
            return nothing

        lax.fori_loop(0, cap // GROUP, group, 0)

    wait_recv(rows_b[:4])
    start(corners_b + rows_b[4:])
    wait_recv(rows_a[4:] + cols_a + corners_a)
    for copy in inner[0]:
        copy.wait()

    def enter(which, slot):
        def before(chunk, rows):
            return times(probe[0, rows], probe[1, rows], window(pad_one, slot, 0, chunk), window(pad_one, slot, 1, chunk))

        def between(rows, re, im):
            return times(wave[0, rows], wave[1, rows], re, im)

        def after(chunk, rows, re, im):
            carry[slot, 0, rows] = re
            carry[slot, 1, rows] = im

        return there_and_back(which, before, between, after)

    frames(enter)

    wait_recv(rows_b[4:] + cols_b + corners_b)
    for copy in inner[1]:
        copy.wait()

    def leave(which, slot):
        def before(chunk, rows):
            second[slot, 0, rows] = window(pad_two, slot, 0, chunk)
            second[slot, 1, rows] = window(pad_two, slot, 1, chunk)
            return times(carry[slot, 0, rows], carry[slot, 1, rows], second[slot, 0, rows], second[slot, 1, rows])

        def between(rows, re, im):
            misfit = re * re + im * im - measured[slot, rows]
            return misfit * re, misfit * im

        def after(chunk, rows, re, im):
            two_re, two_im = conj_times(carry[slot, 0, rows], carry[slot, 1, rows], re, im)
            put(place_two, slot, 0, chunk, two_re)
            put(place_two, slot, 1, chunk, two_im)
            gexit[slot, 0, rows] = re
            gexit[slot, 1, rows] = im

        return there_and_back(which, before, between, after)

    frames(leave)

    blocks = ext // half
    last = blocks - 1

    def gathered(which, comp, row_block, col_block):
        target = slices[which][1]
        value = None
        for slot in range(cap):
            block, _ = column_of(slot)
            moved = col_block - block
            taken = jnp.where(jnp.logical_and(moved >= 0, moved <= 2), moved, 3)
            begin = jnp.clip(row_block * half - offsets[0, slot] + half, 0, 3 * half)
            piece = target[comp, slot, taken, pl.ds(begin, half), :]
            value = piece if value is None else value + piece
        return value

    def block_at(number):
        return pl.ds(pl.multiple_of(number * half, half), half)

    def gather_top(which, first_col, step_col):
        top = slices[which][2]

        def step(number, nothing):
            edge, col_block = number // 2, first_col + number % 2 * step_col
            for comp in range(2):
                top[comp, edge, :, block_at(col_block)] = gathered(which, comp, edge * last, col_block)
            return nothing

        lax.fori_loop(0, 4, step, 0)

    def gather_sides(which):
        side = slices[which][3]

        def step(number, nothing):
            near, row_block = number % 2, number // 2
            for comp in range(2):
                side[comp, near, block_at(row_block), :] = gathered(which, comp, row_block + 1, near * last)
            return nothing

        lax.fori_loop(0, 2 * (blocks - 2), step, 0)

    def gather_inner(which):
        def step(number, nothing):
            row_block, col_block = number // (blocks - 2), number % (blocks - 2)
            for comp in range(2):
                out[2 * which + comp, block_at(row_block), block_at(col_block)] = gathered(
                    which, comp, row_block + 1, col_block + 1
                )
            return nothing

        lax.fori_loop(0, (blocks - 2) * (blocks - 2), step, 0)

    def send_sums(which):
        rows, cols, corners = folds[which]
        gather_top(which, 0, last)
        start(corners)
        gather_top(which, 2, 1)
        start(rows[4:])
        gather_top(which, 1, last - 2)
        gather_sides(which)
        start(cols)
        gather_inner(which)

    def pass_corners(which):
        rows, _, corners = folds[which]
        _, _, top, _, _, land_cols = slices[which]
        wait_recv(corners)
        for edge, band, there in ((0, slice(0, low), has_up), (1, slice(high, ext), has_down)):
            for side, near, cell in ((0, has_left, slice(low, low + half)), (1, has_right, slice(high - half, high))):

                @pl.when(jnp.logical_and(there, near))
                def _():
                    for comp in range(2):
                        top[comp, edge, :, cell] += land_cols[side, comp, band, :]

        start(rows[:4])

    def finish(which):
        rows, cols, _ = folds[which]
        _, _, _, _, land_rows, land_cols = slices[which]
        wait_recv(cols)
        for side, near, cell in ((0, has_left, edge_pieces[0]), (1, has_right, edge_pieces[1])):

            @pl.when(near)
            def _():
                for comp in range(2):
                    out[2 * which + comp, :, cell] += land_cols[side, comp, low:high, :]

        for arrived, pieces in ((rows[4:], (middle,)), (rows[:4], edge_pieces)):
            wait_recv(arrived)
            for side, near, cell in ((0, has_up, edge_pieces[0]), (1, has_down, edge_pieces[1])):

                @pl.when(near)
                def _():
                    for comp in range(2):
                        for piece in pieces:
                            out[2 * which + comp, cell, piece] += land_rows[side, comp, :, piece]

    send_sums(1)

    def back(which, slot):
        def before(chunk, rows):
            return conj_times(second[slot, 0, rows], second[slot, 1, rows], gexit[slot, 0, rows], gexit[slot, 1, rows])

        def between(rows, re, im):
            return conj_times(wave[0, rows], wave[1, rows], re, im)

        def after(chunk, rows, re, im):
            one_re, one_im = conj_times(probe[0, rows], probe[1, rows], re, im)
            put(place_one, slot, 0, chunk, one_re)
            put(place_one, slot, 1, chunk, one_im)

        return there_and_back(which, before, between, after)

    def between_groups(number):
        @pl.when(number == 0)
        def _():
            pass_corners(1)

    frames(back, between_groups)

    send_sums(0)
    pass_corners(0)
    finish(1)
    finish(0)
    wait_send(rows_a[4:] + cols_a + corners_a)
    for exchange in [halos[1], *folds]:
        for copies in exchange:
            wait_send(copies)


def shards(n_gx, n_gy, objects, probe_wave, prop_phase, intensity, offsets, counts):
    frame = intensity.shape[1]
    half = frame // 2
    cap = intensity.shape[0]
    tile = objects.shape[1]
    ext = tile + frame
    anywhere = pl.BlockSpec(memory_space=pl.ANY)
    field = pltpu.VMEM((cap, 2, frame, frame), F32)
    scratch = [
        *[pltpu.VMEM((2, ext // half, ext, half), F32)] * 2,
        *[pltpu.VMEM((2, cap, 4, 4 * half, half), F32)] * 2,
        *[pltpu.VMEM((2, 2, half, ext), F32)] * 2,
        *[pltpu.VMEM((2, 2, tile, half), F32)] * 2,
        *[pltpu.VMEM((2, 2, half, tile), F32)] * 2,
        *[pltpu.VMEM((2, 2, ext, half), F32)] * 2,
        field,
        field,
        field,
        pltpu.VMEM((2, frame, frame), F32),
        pltpu.VMEM((2, frame, frame), F32),
        pltpu.VMEM((cap, frame, frame), F32),
        pltpu.VMEM((6, half, half), F32),
        pltpu.VMEM((frame, frame), F32),
        pltpu.VMEM((4, 3 * frame, frame), BF16),
        pltpu.VMEM((4, frame, 3 * frame), BF16),
        pltpu.VMEM((GROUP, 2, frame, 2 * frame), BF16),
        pltpu.VMEM((GROUP, 2, 2 * frame, frame), BF16),
        pltpu.SMEM((2, cap), jnp.int32),
        pltpu.SMEM((1,), jnp.int32),
        pltpu.SemaphoreType.DMA((4 * COPIES,)),
        pltpu.SemaphoreType.DMA((4 * COPIES,)),
        pltpu.SemaphoreType.DMA((8,)),
        pltpu.SemaphoreType.DMA((2, tile // half)),
    ]
    return pl.pallas_call(
        functools.partial(kernel, n_gx, n_gy),
        out_shape=pltpu.VMEM(objects.shape, F32),
        in_specs=[anywhere] * 7,
        out_specs=pl.BlockSpec(memory_space=pltpu.VMEM),
        scratch_shapes=scratch,
        compiler_params=pltpu.CompilerParams(
            collective_id=0, has_side_effects=True, vmem_limit_bytes=58 * 1024 * 1024
        ),
        name="ptychography",
    )(offsets.T, counts, objects, probe_wave, prop_phase, intensity, jnp.asarray(phase_tables(frame)))


def solution(mesh):
    return jax.shard_map(
        functools.partial(shards, mesh.shape["gx"], mesh.shape["gy"]),
        mesh=mesh,
        in_specs=(
            P(None, "gx", "gy"),
            P(),
            P(),
            P(("gx", "gy"), None, None),
            P(("gx", "gy"), None),
            P(("gx", "gy")),
        ),
        out_specs=P(None, "gx", "gy"),
        check_vma=False,
    )
```

```python
import functools

import jax
import jax.numpy as jnp
import numpy as np
from jax import lax
from jax.experimental import pallas as pl
from jax.experimental.pallas import tpu as pltpu
from jax.sharding import PartitionSpec as P

F32 = jnp.float32
BF16 = jnp.bfloat16
MESH = pl.DeviceIdType.MESH
CHUNK = 64
COPIES = 14
GROUP = 2
steps_end = object()


def phase_tables(frame_len):
    half = frame_len // 2
    n = np.arange(half)[:, None]
    k = np.arange(half)[None, :]
    factor = 1.0 / np.sqrt(frame_len)
    even = 2.0 * np.pi * (n * 2 * k % frame_len) / frame_len
    odd = 2.0 * np.pi * (n * (2 * k + 1) % frame_len) / frame_len
    parts = [np.cos(even), np.sin(even), np.cos(odd), np.sin(odd), np.cos(odd).T, np.sin(odd).T]
    return np.stack([part * factor for part in parts]).astype(np.float32)


def split(value):
    high = value.astype(BF16)
    return high, (value - high.astype(F32)).astype(BF16)


def dot(left, right):
    return jnp.dot(left, right, preferred_element_type=F32)


def times(left_re, left_im, right_re, right_im):
    return left_re * right_re - left_im * right_im, left_re * right_im + left_im * right_re


def conj_times(left_re, left_im, right_re, right_im):
    return left_re * right_re + left_im * right_im, left_re * right_im - left_im * right_re


def kernel(
    n_gx, n_gy, offsets_hbm, counts_hbm, objects, probe_hbm, phase_hbm, intensity_hbm, tables_hbm, out,
    pad_one, pad_two, place_one, place_two, top_one, top_two, side_one, side_two, rows_one, rows_two, cols_one, cols_two,
    carry, second, gexit, probe, wave, measured, tables, phase, weights_r, weights_l, rows_in, cols_in,
    offsets, counts, send_sem, recv_sem, local_sem, inner_sem,
):
    frame = probe.shape[1]
    half = frame // 2
    cap = intensity_hbm.shape[0]
    tile = objects.shape[1]
    ext = tile + frame
    low, high = half, half + tile
    gx, gy = lax.axis_index("gx"), lax.axis_index("gy")
    has_up, has_down = gx > 0, gx < n_gx - 1
    has_left, has_right = gy > 0, gy < n_gy - 1
    up, down, left, right = (gx - 1, gy), (gx + 1, gy), (gx, gy - 1), (gx, gy + 1)
    slices = (
        (pad_one, place_one, top_one, side_one, rows_one, cols_one),
        (pad_two, place_two, top_two, side_two, rows_two, cols_two),
    )

    barrier = pltpu.get_barrier_semaphore()
    sides = ((has_up, up), (has_down, down), (has_left, left), (has_right, right))
    for there, device in sides:

        @pl.when(there)
        def _():
            pl.semaphore_signal(barrier, inc=1, device_id=device, device_id_type=MESH)

    local = [
        pltpu.make_async_copy(tables_hbm, tables, local_sem.at[0]),
        pltpu.make_async_copy(phase_hbm, phase, local_sem.at[1]),
        pltpu.make_async_copy(intensity_hbm, measured, local_sem.at[2]),
        pltpu.make_async_copy(probe_hbm, probe, local_sem.at[3]),
        pltpu.make_async_copy(offsets_hbm, offsets, local_sem.at[4]),
        pltpu.make_async_copy(counts_hbm, counts, local_sem.at[5]),
    ]
    inner = [
        [
            pltpu.make_async_copy(
                objects.at[2 * which : 2 * which + 2, :, block * half : (block + 1) * half],
                pad.at[:, block + 1, low:high],
                inner_sem.at[which, block],
            )
            for block in range(tile // half)
        ]
        for which, pad in enumerate((pad_one, pad_two))
    ]
    local += inner[0] + inner[1]
    for copy in local[:3]:
        copy.start()

    pl.semaphore_wait(barrier, sum(there.astype(jnp.int32) for there, _ in sides))

    def remote(number, source, target, device, sends, receives):
        copy = pltpu.make_async_remote_copy(
            src_ref=source, dst_ref=target, send_sem=send_sem.at[number], recv_sem=recv_sem.at[number],
            device_id=device, device_id_type=MESH,
        )
        return sends, receives, copy

    def start(copies):
        for sends, _, copy in copies:
            pl.when(sends)(copy.start)

    def wait_recv(copies):
        for _, receives, copy in copies:
            pl.when(receives)(copy.wait_recv)

    def wait_send(copies):
        for sends, _, copy in copies:
            pl.when(sends)(copy.wait_send)

    edge_pieces = (slice(0, half), slice(tile - half, tile))
    middle = slice(half, tile - half)

    def shift_by(piece, distance):
        return slice(piece.start + distance, piece.stop + distance)

    def halo(which):
        pad = slices[which][0]
        cells = objects.at[2 * which : 2 * which + 2]
        base = which * COPIES
        rows = []
        blocks = tile // half
        for block in (0, blocks - 1, *range(1, blocks - 1)):
            piece = slice(block * half, (block + 1) * half)
            rows.append(
                remote(base + len(rows), cells.at[:, 0:half, piece], pad.at[:, block + 1, high:ext], up, has_up, has_down)
            )
            rows.append(
                remote(base + len(rows), cells.at[:, tile - half : tile, piece], pad.at[:, block + 1, 0:low], down, has_down, has_up)
            )
        cols = [
            remote(base + 8, cells.at[:, :, 0:half], pad.at[:, blocks + 1, low:high], left, has_left, has_right),
            remote(base + 9, cells.at[:, :, tile - half : tile], pad.at[:, 0, low:high], right, has_right, has_left),
        ]
        corners = []
        for band, there in ((slice(0, low), has_up), (slice(high, ext), has_down)):
            to_left, to_right = jnp.logical_and(there, has_left), jnp.logical_and(there, has_right)
            corners.append(
                remote(base + 10 + len(corners), pad.at[:, 1, band], pad.at[:, blocks + 1, band], left, to_left, to_right)
            )
            corners.append(
                remote(base + 10 + len(corners), pad.at[:, blocks, band], pad.at[:, 0, band], right, to_right, to_left)
            )
        return rows, cols, corners

    def fold(which):
        _, _, top, side, land_rows, land_cols = slices[which]
        base = (2 + which) * COPIES
        rows = []
        for piece in (*edge_pieces, middle):
            moved = shift_by(piece, half)
            rows.append(
                remote(base + len(rows), top.at[:, 0, :, moved], land_rows.at[1, :, :, piece], up, has_up, has_down)
            )
            rows.append(
                remote(base + len(rows), top.at[:, 1, :, moved], land_rows.at[0, :, :, piece], down, has_down, has_up)
            )
        cols = [
            remote(base + 6, side.at[:, 0], land_cols.at[1, :, low:high], left, has_left, has_right),
            remote(base + 7, side.at[:, 1], land_cols.at[0, :, low:high], right, has_right, has_left),
        ]
        corners = []
        for edge, band, there in ((0, slice(0, low), has_up), (1, slice(high, ext), has_down)):
            to_left, to_right = jnp.logical_and(there, has_left), jnp.logical_and(there, has_right)
            corners.append(
                remote(base + 8 + len(corners), top.at[:, edge, :, 0:low], land_cols.at[1, :, band], left, to_left, to_right)
            )
            corners.append(
                remote(base + 8 + len(corners), top.at[:, edge, :, high:ext], land_cols.at[0, :, band], right, to_right, to_left)
            )
        return rows, cols, corners

    halos = [halo(0), halo(1)]
    folds = [fold(0), fold(1)]

    (rows_a, cols_a, corners_a), (rows_b, cols_b, corners_b) = halos
    start(rows_a[:4] + rows_b[:4] + cols_a)
    for copy in local[3:]:
        copy.start()

    for pad in (pad_one, pad_two):

        @pl.when(jnp.logical_not(has_up))
        def _():
            pad[:, :, 0:low] = jnp.zeros((2, ext // half, low, half), F32)

        @pl.when(jnp.logical_not(has_down))
        def _():
            pad[:, :, high:ext] = jnp.zeros((2, ext // half, low, half), F32)

        @pl.when(jnp.logical_not(has_left))
        def _():
            pad[:, 0] = jnp.zeros((2, ext, half), F32)

        @pl.when(jnp.logical_not(has_right))
        def _():
            pad[:, ext // half - 1] = jnp.zeros((2, ext, half), F32)

    local[0].wait()
    cos_e, sin_e, cos_o, sin_o, cos_t, sin_t = (tables[i] for i in range(6))

    def real_form(cosine, sine):
        return jnp.concatenate([jnp.concatenate([cosine, -sine], 1), jnp.concatenate([sine, cosine], 1)], 0)

    forms = (real_form(cos_e, sin_e), real_form(cos_o, sin_o), real_form(cos_e, -sin_e), real_form(cos_t, -sin_t))
    for number, form in enumerate(forms):
        top, rest = split(form)
        for part, value in enumerate((top, top, rest)):
            weights_r[number, part * frame : (part + 1) * frame, :] = value
            weights_l[number, :, part * frame : (part + 1) * frame] = value

    place = lax.broadcasted_iota(jnp.int32, (frame, frame), 0)
    other = lax.broadcasted_iota(jnp.int32, (frame, frame), 1)

    def picked(i):
        return jnp.where(i < half, 2 * i, 2 * (i - half) + 1)

    pick_rows = jnp.where(other == picked(place), 1.0, 0.0).astype(BF16)
    pick_cols = jnp.where(place == picked(other), 1.0, 0.0).astype(BF16)

    def sorted_frequencies(value):
        for axis in (0, 1):
            top, rest = split(value)
            middle_part, last = split(value - top.astype(F32))
            del rest
            parts = (top, middle_part, last)
            if axis == 0:
                value = sum(dot(pick_rows, part) for part in parts[::-1])
            else:
                value = sum(dot(part, pick_cols) for part in parts[::-1])
        return value

    local[1].wait()
    angle = sorted_frequencies(phase[...])
    wave[0] = jnp.cos(angle)
    wave[1] = jnp.sin(angle)
    wait_send(rows_a[:4])
    start(rows_a[4:] + cols_b)
    local[2].wait()

    def sort_slot(slot, nothing):
        measured[slot] = sorted_frequencies(measured[slot])
        return nothing

    lax.fori_loop(0, cap, sort_slot, 0)

    wait_recv(rows_a[:4])
    start(corners_a)

    def clear_place(slot, nothing):
        for target in (place_one, place_two):
            for comp in range(2):
                target[comp, slot, 3] = jnp.zeros((4 * half, half), F32)
                for block in range(3):
                    target[comp, slot, block, 0:half] = jnp.zeros((half, half), F32)
                    target[comp, slot, block, 3 * half : 4 * half] = jnp.zeros((half, half), F32)
        return nothing

    lax.fori_loop(0, cap, clear_place, 0)
    local[3].wait()
    local[4].wait()
    local[5].wait()

    lane = lax.broadcasted_iota(jnp.int32, (CHUNK, half), 1)

    def column_of(slot):
        column = offsets[1, slot]
        block = jnp.minimum(column // half, tile // half - 1)
        return block, column - block * half

    def window(pad, slot, comp, chunk):
        row = offsets[0, slot]
        block, shift = column_of(slot)
        rows = pl.ds(row + chunk * CHUNK, CHUNK)
        back = jnp.where(jnp.logical_or(shift == 0, shift == half), 0, half - shift)
        turned = [pltpu.roll(pad[comp, block + i, rows, :], back, 1) for i in range(3)]
        kept = lane < half - shift
        return jnp.concatenate([jnp.where(kept, turned[i], turned[i + 1]) for i in range(2)], 1)

    def put(target, slot, comp, chunk, value):
        _, shift = column_of(slot)
        turn = jnp.where(shift == half, 0, shift)
        value = jnp.where(slot < counts[0], value, jnp.zeros_like(value))
        first = pltpu.roll(value[:, :half], turn, 1)
        last = pltpu.roll(value[:, half:], turn, 1)
        inside = lane >= shift
        nothing = jnp.zeros_like(first)
        rows = slice(half + chunk * CHUNK, half + (chunk + 1) * CHUNK)
        target[comp, slot, 0, rows] = jnp.where(inside, first, nothing)
        target[comp, slot, 1, rows] = jnp.where(inside, last, first)
        target[comp, slot, 2, rows] = jnp.where(inside, nothing, last)

    def right_dot(lane_of, j, number):
        value = rows_in[lane_of, j]
        return dot(jnp.concatenate([value, value[:, :frame]], 1), weights_r[number])

    def left_dot(lane_of, i, number):
        value = cols_in[lane_of, i]
        return dot(weights_l[number], jnp.concatenate([value, value[:frame]], 0))

    def there_and_back(which, before, between, after):
        chunks = [slice(c * CHUNK, (c + 1) * CHUNK) for c in range(frame // CHUNK)]
        for c, rows in enumerate(chunks):
            re, im = before(c, rows)
            for j in range(2):
                if j == 0:
                    mixed = jnp.concatenate([re[:, :half] + re[:, half:], im[:, :half] + im[:, half:]], 1)
                else:
                    mixed = jnp.concatenate([re[:, :half] - re[:, half:], im[:, :half] - im[:, half:]], 1)
                top, rest = split(mixed)
                rows_in[which, j, rows, 0:frame] = top
                rows_in[which, j, rows, frame : 2 * frame] = rest
        yield
        for j in range(2):
            value = right_dot(which, j, j)
            cols = slice(j * half, (j + 1) * half)
            for i in range(2):
                mixed = value[:half] + value[half:] if i == 0 else value[:half] - value[half:]
                for part, piece in enumerate(split(mixed)):
                    cols_in[which, i, part * frame : part * frame + half, cols] = piece[:, :half]
                    cols_in[which, i, part * frame + half : (part + 1) * frame, cols] = piece[:, half:]
        yield
        for i in range(2):
            value = left_dot(which, i, 2 + i)
            re, im = between(slice(i * half, (i + 1) * half), value[:half], value[half:])
            for position, field in enumerate((re, im)):
                for part, piece in enumerate(split(field)):
                    begin = part * frame + position * half
                    cols_in[which, i, begin : begin + half, :] = piece
        yield
        even, odd = left_dot(which, 0, 0), left_dot(which, 1, 1)
        for i in range(2):
            mixed = even + odd if i == 0 else even - odd
            rows = slice(i * half, (i + 1) * half)
            for j in range(2):
                for part, piece in enumerate(split(mixed[:, j * half : (j + 1) * half])):
                    begin = part * frame
                    rows_in[which, j, rows, begin : begin + half] = piece[:half]
                    rows_in[which, j, rows, begin + half : begin + frame] = piece[half:]
        yield
        even, odd = right_dot(which, 0, 2), right_dot(which, 1, 3)
        total, difference = even + odd, even - odd
        for c, rows in enumerate(chunks):
            re = jnp.concatenate([total[rows, :half], difference[rows, :half]], 1)
            im = jnp.concatenate([total[rows, half:], difference[rows, half:]], 1)
            after(c, rows, re, im)

    def frames(steps_of, then=None, at_once=False):
        def group(number, nothing):
            running = [steps_of(which, number * GROUP + which) for which in range(GROUP)]
            while running:
                running = [steps for steps in running if next(steps, steps_end) is not steps_end]
            if then is not None:
                then(number)
            return nothing

        if at_once:
            running = [steps_of(which, which) for which in range(cap)]
            while running:
                running = [steps for steps in running if next(steps, steps_end) is not steps_end]
        else:
            lax.fori_loop(0, cap // GROUP, group, 0)

    wait_recv(rows_b[:4])
    start(corners_b + rows_b[4:])
    wait_recv(rows_a[4:] + cols_a + corners_a)
    for copy in inner[0]:
        copy.wait()

    def enter(which, slot):
        def before(chunk, rows):
            return times(probe[0, rows], probe[1, rows], window(pad_one, slot, 0, chunk), window(pad_one, slot, 1, chunk))

        def between(rows, re, im):
            return times(wave[0, rows], wave[1, rows], re, im)

        def after(chunk, rows, re, im):
            carry[slot, 0, rows] = re
            carry[slot, 1, rows] = im

        return there_and_back(which, before, between, after)

    frames(enter)

    wait_recv(rows_b[4:] + cols_b + corners_b)
    for copy in inner[1]:
        copy.wait()

    def leave(which, slot):
        def before(chunk, rows):
            second[slot, 0, rows] = window(pad_two, slot, 0, chunk)
            second[slot, 1, rows] = window(pad_two, slot, 1, chunk)
            return times(carry[slot, 0, rows], carry[slot, 1, rows], second[slot, 0, rows], second[slot, 1, rows])

        def between(rows, re, im):
            misfit = re * re + im * im - measured[slot, rows]
            return misfit * re, misfit * im

        def after(chunk, rows, re, im):
            two_re, two_im = conj_times(carry[slot, 0, rows], carry[slot, 1, rows], re, im)
            put(place_two, slot, 0, chunk, two_re)
            put(place_two, slot, 1, chunk, two_im)
            gexit[slot, 0, rows] = re
            gexit[slot, 1, rows] = im

        return there_and_back(which, before, between, after)

    frames(leave, at_once=True)

    blocks = ext // half
    last = blocks - 1

    def gathered(which, comp, row_block, col_block):
        target = slices[which][1]
        value = None
        for slot in range(cap):
            block, _ = column_of(slot)
            moved = col_block - block
            taken = jnp.where(jnp.logical_and(moved >= 0, moved <= 2), moved, 3)
            begin = jnp.clip(row_block * half - offsets[0, slot] + half, 0, 3 * half)
            piece = target[comp, slot, taken, pl.ds(begin, half), :]
            value = piece if value is None else value + piece
        return value

    def block_at(number):
        return pl.ds(pl.multiple_of(number * half, half), half)

    def gather_top(which, first_col, step_col):
        top = slices[which][2]

        def step(number, nothing):
            edge, col_block = number // 2, first_col + number % 2 * step_col
            for comp in range(2):
                top[comp, edge, :, block_at(col_block)] = gathered(which, comp, edge * last, col_block)
            return nothing

        lax.fori_loop(0, 4, step, 0)

    def gather_sides(which):
        side = slices[which][3]

        def step(number, nothing):
            near, row_block = number % 2, number // 2
            for comp in range(2):
                side[comp, near, block_at(row_block), :] = gathered(which, comp, row_block + 1, near * last)
            return nothing

        lax.fori_loop(0, 2 * (blocks - 2), step, 0)

    def gather_inner(which):
        def step(number, nothing):
            row_block, col_block = number // (blocks - 2), number % (blocks - 2)
            for comp in range(2):
                out[2 * which + comp, block_at(row_block), block_at(col_block)] = gathered(
                    which, comp, row_block + 1, col_block + 1
                )
            return nothing

        lax.fori_loop(0, (blocks - 2) * (blocks - 2), step, 0)

    def send_sums(which):
        rows, cols, corners = folds[which]
        gather_top(which, 2, 1)
        start(rows[4:])
        gather_top(which, 0, last)
        start(corners)
        gather_top(which, 1, last - 2)
        gather_sides(which)
        start(cols)
        gather_inner(which)

    def pass_corners(which):
        rows, _, corners = folds[which]
        _, _, top, _, _, land_cols = slices[which]
        wait_recv(corners)
        for edge, band, there in ((0, slice(0, low), has_up), (1, slice(high, ext), has_down)):
            for side, near, cell in ((0, has_left, slice(low, low + half)), (1, has_right, slice(high - half, high))):

                @pl.when(jnp.logical_and(there, near))
                def _():
                    for comp in range(2):
                        top[comp, edge, :, cell] += land_cols[side, comp, band, :]

        start(rows[:4])

    def finish(which):
        rows, cols, _ = folds[which]
        _, _, _, _, land_rows, land_cols = slices[which]
        wait_recv(cols)
        for side, near, cell in ((0, has_left, edge_pieces[0]), (1, has_right, edge_pieces[1])):

            @pl.when(near)
            def _():
                for comp in range(2):
                    out[2 * which + comp, :, cell] += land_cols[side, comp, low:high, :]

        for arrived, pieces in ((rows[4:], (middle,)), (rows[:4], edge_pieces)):
            wait_recv(arrived)
            for side, near, cell in ((0, has_up, edge_pieces[0]), (1, has_down, edge_pieces[1])):

                @pl.when(near)
                def _():
                    for comp in range(2):
                        for piece in pieces:
                            out[2 * which + comp, cell, piece] += land_rows[side, comp, :, piece]

    send_sums(1)

    def back(which, slot):
        def before(chunk, rows):
            return conj_times(second[slot, 0, rows], second[slot, 1, rows], gexit[slot, 0, rows], gexit[slot, 1, rows])

        def between(rows, re, im):
            return conj_times(wave[0, rows], wave[1, rows], re, im)

        def after(chunk, rows, re, im):
            one_re, one_im = conj_times(probe[0, rows], probe[1, rows], re, im)
            put(place_one, slot, 0, chunk, one_re)
            put(place_one, slot, 1, chunk, one_im)

        return there_and_back(which, before, between, after)

    def between_groups(number):
        @pl.when(number == 0)
        def _():
            pass_corners(1)

    frames(back, between_groups)

    send_sums(0)
    pass_corners(0)
    finish(1)
    finish(0)
    wait_send(rows_a[4:] + cols_a + corners_a)
    for exchange in [halos[1], *folds]:
        for copies in exchange:
            wait_send(copies)


def shards(n_gx, n_gy, objects, probe_wave, prop_phase, intensity, offsets, counts):
    frame = intensity.shape[1]
    half = frame // 2
    cap = intensity.shape[0]
    tile = objects.shape[1]
    ext = tile + frame
    anywhere = pl.BlockSpec(memory_space=pl.ANY)
    field = pltpu.VMEM((cap, 2, frame, frame), F32)
    scratch = [
        *[pltpu.VMEM((2, ext // half, ext, half), F32)] * 2,
        *[pltpu.VMEM((2, cap, 4, 4 * half, half), F32)] * 2,
        *[pltpu.VMEM((2, 2, half, ext), F32)] * 2,
        *[pltpu.VMEM((2, 2, tile, half), F32)] * 2,
        *[pltpu.VMEM((2, 2, half, tile), F32)] * 2,
        *[pltpu.VMEM((2, 2, ext, half), F32)] * 2,
        field,
        field,
        field,
        pltpu.VMEM((2, frame, frame), F32),
        pltpu.VMEM((2, frame, frame), F32),
        pltpu.VMEM((cap, frame, frame), F32),
        pltpu.VMEM((6, half, half), F32),
        pltpu.VMEM((frame, frame), F32),
        pltpu.VMEM((4, 3 * frame, frame), BF16),
        pltpu.VMEM((4, frame, 3 * frame), BF16),
        pltpu.VMEM((cap, 2, frame, 2 * frame), BF16),
        pltpu.VMEM((cap, 2, 2 * frame, frame), BF16),
        pltpu.SMEM((2, cap), jnp.int32),
        pltpu.SMEM((1,), jnp.int32),
        pltpu.SemaphoreType.DMA((4 * COPIES,)),
        pltpu.SemaphoreType.DMA((4 * COPIES,)),
        pltpu.SemaphoreType.DMA((8,)),
        pltpu.SemaphoreType.DMA((2, tile // half)),
    ]
    return pl.pallas_call(
        functools.partial(kernel, n_gx, n_gy),
        out_shape=pltpu.VMEM(objects.shape, F32),
        in_specs=[anywhere] * 7,
        out_specs=pl.BlockSpec(memory_space=pltpu.VMEM),
        scratch_shapes=scratch,
        compiler_params=pltpu.CompilerParams(
            collective_id=0, has_side_effects=True, vmem_limit_bytes=58 * 1024 * 1024
        ),
        name="ptychography",
    )(offsets.T, counts, objects, probe_wave, prop_phase, intensity, jnp.asarray(phase_tables(frame)))


def solution(mesh):
    return jax.shard_map(
        functools.partial(shards, mesh.shape["gx"], mesh.shape["gy"]),
        mesh=mesh,
        in_specs=(
            P(None, "gx", "gy"),
            P(),
            P(),
            P(("gx", "gy"), None, None),
            P(("gx", "gy"), None),
            P(("gx", "gy")),
        ),
        out_specs=P(None, "gx", "gy"),
        check_vma=False,
    )
```

```python
import functools

import jax
import jax.numpy as jnp
import numpy as np
from jax import lax
from jax.experimental import pallas as pl
from jax.experimental.pallas import tpu as pltpu
from jax.sharding import PartitionSpec as P

F32 = jnp.float32
BF16 = jnp.bfloat16
MESH = pl.DeviceIdType.MESH
CHUNK = 64
COPIES = 14
GROUP = 2
steps_end = object()


def phase_tables(frame_len):
    half = frame_len // 2
    n = np.arange(half)[:, None]
    k = np.arange(half)[None, :]
    factor = 1.0 / np.sqrt(frame_len)
    even = 2.0 * np.pi * (n * 2 * k % frame_len) / frame_len
    odd = 2.0 * np.pi * (n * (2 * k + 1) % frame_len) / frame_len
    parts = [np.cos(even), np.sin(even), np.cos(odd), np.sin(odd), np.cos(odd).T, np.sin(odd).T]
    return np.stack([part * factor for part in parts]).astype(np.float32)


def split(value):
    high = value.astype(BF16)
    return high, (value - high.astype(F32)).astype(BF16)


def dot(left, right):
    return jnp.dot(left, right, preferred_element_type=F32)


def times(left_re, left_im, right_re, right_im):
    return left_re * right_re - left_im * right_im, left_re * right_im + left_im * right_re


def conj_times(left_re, left_im, right_re, right_im):
    return left_re * right_re + left_im * right_im, left_re * right_im - left_im * right_re


def kernel(
    n_gx, n_gy, offsets_hbm, counts_hbm, objects, probe_hbm, phase_hbm, intensity_hbm, tables_hbm, out,
    pad_one, pad_two, place_one, place_two, top_one, top_two, side_one, side_two, rows_one, rows_two, cols_one, cols_two,
    carry, second, gexit, probe, wave, measured, tables, phase, weights_r, weights_l, rows_in, cols_in,
    offsets, counts, send_sem, recv_sem, local_sem, inner_sem,
):
    frame = probe.shape[1]
    half = frame // 2
    cap = intensity_hbm.shape[0]
    tile = objects.shape[1]
    ext = tile + frame
    low, high = half, half + tile
    gx, gy = lax.axis_index("gx"), lax.axis_index("gy")
    has_up, has_down = gx > 0, gx < n_gx - 1
    has_left, has_right = gy > 0, gy < n_gy - 1
    up, down, left, right = (gx - 1, gy), (gx + 1, gy), (gx, gy - 1), (gx, gy + 1)
    slices = (
        (pad_one, place_one, top_one, side_one, rows_one, cols_one),
        (pad_two, place_two, top_two, side_two, rows_two, cols_two),
    )

    barrier = pltpu.get_barrier_semaphore()
    sides = ((has_up, up), (has_down, down), (has_left, left), (has_right, right))
    for there, device in sides:

        @pl.when(there)
        def _():
            pl.semaphore_signal(barrier, inc=1, device_id=device, device_id_type=MESH)

    local = [
        pltpu.make_async_copy(tables_hbm, tables, local_sem.at[0]),
        pltpu.make_async_copy(phase_hbm, phase, local_sem.at[1]),
        pltpu.make_async_copy(intensity_hbm, measured, local_sem.at[2]),
        pltpu.make_async_copy(probe_hbm, probe, local_sem.at[3]),
        pltpu.make_async_copy(offsets_hbm, offsets, local_sem.at[4]),
        pltpu.make_async_copy(counts_hbm, counts, local_sem.at[5]),
    ]
    inner = [
        [
            pltpu.make_async_copy(
                objects.at[2 * which : 2 * which + 2, :, block * half : (block + 1) * half],
                pad.at[:, block + 1, low:high],
                inner_sem.at[which, block],
            )
            for block in range(tile // half)
        ]
        for which, pad in enumerate((pad_one, pad_two))
    ]
    local += inner[0] + inner[1]
    for copy in local[:3]:
        copy.start()

    pl.semaphore_wait(barrier, sum(there.astype(jnp.int32) for there, _ in sides))

    def remote(number, source, target, device, sends, receives):
        copy = pltpu.make_async_remote_copy(
            src_ref=source, dst_ref=target, send_sem=send_sem.at[number], recv_sem=recv_sem.at[number],
            device_id=device, device_id_type=MESH,
        )
        return sends, receives, copy

    def start(copies):
        for sends, _, copy in copies:
            pl.when(sends)(copy.start)

    def wait_recv(copies):
        for _, receives, copy in copies:
            pl.when(receives)(copy.wait_recv)

    def wait_send(copies):
        for sends, _, copy in copies:
            pl.when(sends)(copy.wait_send)

    edge_pieces = (slice(0, half), slice(tile - half, tile))
    middle = slice(half, tile - half)

    def shift_by(piece, distance):
        return slice(piece.start + distance, piece.stop + distance)

    def halo(which):
        pad = slices[which][0]
        cells = objects.at[2 * which : 2 * which + 2]
        base = which * COPIES
        rows = []
        blocks = tile // half
        for block in (0, blocks - 1, *range(1, blocks - 1)):
            piece = slice(block * half, (block + 1) * half)
            rows.append(
                remote(base + len(rows), cells.at[:, 0:half, piece], pad.at[:, block + 1, high:ext], up, has_up, has_down)
            )
            rows.append(
                remote(base + len(rows), cells.at[:, tile - half : tile, piece], pad.at[:, block + 1, 0:low], down, has_down, has_up)
            )
        cols = [
            remote(base + 8, cells.at[:, :, 0:half], pad.at[:, blocks + 1, low:high], left, has_left, has_right),
            remote(base + 9, cells.at[:, :, tile - half : tile], pad.at[:, 0, low:high], right, has_right, has_left),
        ]
        corners = []
        for band, there in ((slice(0, low), has_up), (slice(high, ext), has_down)):
            to_left, to_right = jnp.logical_and(there, has_left), jnp.logical_and(there, has_right)
            corners.append(
                remote(base + 10 + len(corners), pad.at[:, 1, band], pad.at[:, blocks + 1, band], left, to_left, to_right)
            )
            corners.append(
                remote(base + 10 + len(corners), pad.at[:, blocks, band], pad.at[:, 0, band], right, to_right, to_left)
            )
        return rows, cols, corners

    def fold(which):
        _, _, top, side, land_rows, land_cols = slices[which]
        base = (2 + which) * COPIES
        rows = []
        for piece in (*edge_pieces, middle):
            moved = shift_by(piece, half)
            rows.append(
                remote(base + len(rows), top.at[:, 0, :, moved], land_rows.at[1, :, :, piece], up, has_up, has_down)
            )
            rows.append(
                remote(base + len(rows), top.at[:, 1, :, moved], land_rows.at[0, :, :, piece], down, has_down, has_up)
            )
        cols = [
            remote(base + 6, side.at[:, 0], land_cols.at[1, :, low:high], left, has_left, has_right),
            remote(base + 7, side.at[:, 1], land_cols.at[0, :, low:high], right, has_right, has_left),
        ]
        corners = []
        for edge, band, there in ((0, slice(0, low), has_up), (1, slice(high, ext), has_down)):
            to_left, to_right = jnp.logical_and(there, has_left), jnp.logical_and(there, has_right)
            corners.append(
                remote(base + 8 + len(corners), top.at[:, edge, :, 0:low], land_cols.at[1, :, band], left, to_left, to_right)
            )
            corners.append(
                remote(base + 8 + len(corners), top.at[:, edge, :, high:ext], land_cols.at[0, :, band], right, to_right, to_left)
            )
        return rows, cols, corners

    halos = [halo(0), halo(1)]
    folds = [fold(0), fold(1)]

    (rows_a, cols_a, corners_a), (rows_b, cols_b, corners_b) = halos
    start(rows_a[:4] + rows_b[:4] + cols_a)
    for copy in local[3:]:
        copy.start()

    for pad in (pad_one, pad_two):

        @pl.when(jnp.logical_not(has_up))
        def _():
            pad[:, :, 0:low] = jnp.zeros((2, ext // half, low, half), F32)

        @pl.when(jnp.logical_not(has_down))
        def _():
            pad[:, :, high:ext] = jnp.zeros((2, ext // half, low, half), F32)

        @pl.when(jnp.logical_not(has_left))
        def _():
            pad[:, 0] = jnp.zeros((2, ext, half), F32)

        @pl.when(jnp.logical_not(has_right))
        def _():
            pad[:, ext // half - 1] = jnp.zeros((2, ext, half), F32)

    local[0].wait()
    cos_e, sin_e, cos_o, sin_o, cos_t, sin_t = (tables[i] for i in range(6))

    def real_form(cosine, sine):
        return jnp.concatenate([jnp.concatenate([cosine, -sine], 1), jnp.concatenate([sine, cosine], 1)], 0)

    forms = (real_form(cos_e, sin_e), real_form(cos_o, sin_o), real_form(cos_e, -sin_e), real_form(cos_t, -sin_t))
    for number, form in enumerate(forms):
        top, rest = split(form)
        for part, value in enumerate((top, top, rest)):
            weights_r[number, part * frame : (part + 1) * frame, :] = value
            weights_l[number, :, part * frame : (part + 1) * frame] = value

    place = lax.broadcasted_iota(jnp.int32, (frame, frame), 0)
    other = lax.broadcasted_iota(jnp.int32, (frame, frame), 1)

    def picked(i):
        return jnp.where(i < half, 2 * i, 2 * (i - half) + 1)

    pick_rows = jnp.where(other == picked(place), 1.0, 0.0).astype(BF16)
    pick_cols = jnp.where(place == picked(other), 1.0, 0.0).astype(BF16)

    def sorted_frequencies(value):
        for axis in (0, 1):
            top, rest = split(value)
            middle_part, last = split(value - top.astype(F32))
            del rest
            parts = (top, middle_part, last)
            if axis == 0:
                value = sum(dot(pick_rows, part) for part in parts[::-1])
            else:
                value = sum(dot(part, pick_cols) for part in parts[::-1])
        return value

    local[1].wait()
    angle = sorted_frequencies(phase[...])
    wave[0] = jnp.cos(angle)
    wave[1] = jnp.sin(angle)
    wait_send(rows_a[:4])
    start(rows_a[4:] + cols_b)
    local[2].wait()

    def sort_slot(slot, nothing):
        measured[slot] = sorted_frequencies(measured[slot])
        return nothing

    lax.fori_loop(0, cap, sort_slot, 0)

    wait_recv(rows_a[:4])
    start(corners_a)

    def clear_place(slot, nothing):
        for target in (place_one, place_two):
            for comp in range(2):
                target[comp, slot, 3] = jnp.zeros((4 * half, half), F32)
                for block in range(3):
                    target[comp, slot, block, 0:half] = jnp.zeros((half, half), F32)
                    target[comp, slot, block, 3 * half : 4 * half] = jnp.zeros((half, half), F32)
        return nothing

    lax.fori_loop(0, cap, clear_place, 0)
    local[3].wait()
    local[4].wait()
    local[5].wait()

    lane = lax.broadcasted_iota(jnp.int32, (CHUNK, half), 1)

    def column_of(slot):
        column = offsets[1, slot]
        block = jnp.minimum(column // half, tile // half - 1)
        return block, column - block * half

    def window(pad, slot, comp, chunk):
        row = offsets[0, slot]
        block, shift = column_of(slot)
        rows = pl.ds(row + chunk * CHUNK, CHUNK)
        back = jnp.where(jnp.logical_or(shift == 0, shift == half), 0, half - shift)
        turned = [pltpu.roll(pad[comp, block + i, rows, :], back, 1) for i in range(3)]
        kept = lane < half - shift
        return jnp.concatenate([jnp.where(kept, turned[i], turned[i + 1]) for i in range(2)], 1)

    def put(target, slot, comp, chunk, value):
        _, shift = column_of(slot)
        turn = jnp.where(shift == half, 0, shift)
        value = jnp.where(slot < counts[0], value, jnp.zeros_like(value))
        first = pltpu.roll(value[:, :half], turn, 1)
        last = pltpu.roll(value[:, half:], turn, 1)
        inside = lane >= shift
        nothing = jnp.zeros_like(first)
        rows = slice(half + chunk * CHUNK, half + (chunk + 1) * CHUNK)
        target[comp, slot, 0, rows] = jnp.where(inside, first, nothing)
        target[comp, slot, 1, rows] = jnp.where(inside, last, first)
        target[comp, slot, 2, rows] = jnp.where(inside, nothing, last)

    def right_dot(lane_of, j, number):
        value = rows_in[lane_of, j]
        return dot(jnp.concatenate([value, value[:, :frame]], 1), weights_r[number])

    def left_dot(lane_of, i, number):
        value = cols_in[lane_of, i]
        return dot(weights_l[number], jnp.concatenate([value, value[:frame]], 0))

    def there_and_back(which, before, between, after):
        chunks = [slice(c * CHUNK, (c + 1) * CHUNK) for c in range(frame // CHUNK)]
        for c, rows in enumerate(chunks):
            re, im = before(c, rows)
            for j in range(2):
                if j == 0:
                    mixed = jnp.concatenate([re[:, :half] + re[:, half:], im[:, :half] + im[:, half:]], 1)
                else:
                    mixed = jnp.concatenate([re[:, :half] - re[:, half:], im[:, :half] - im[:, half:]], 1)
                top, rest = split(mixed)
                rows_in[which, j, rows, 0:frame] = top
                rows_in[which, j, rows, frame : 2 * frame] = rest
        yield
        for j in range(2):
            value = right_dot(which, j, j)
            cols = slice(j * half, (j + 1) * half)
            for i in range(2):
                mixed = value[:half] + value[half:] if i == 0 else value[:half] - value[half:]
                for part, piece in enumerate(split(mixed)):
                    cols_in[which, i, part * frame : part * frame + half, cols] = piece[:, :half]
                    cols_in[which, i, part * frame + half : (part + 1) * frame, cols] = piece[:, half:]
        yield
        for i in range(2):
            value = left_dot(which, i, 2 + i)
            re, im = between(slice(i * half, (i + 1) * half), value[:half], value[half:])
            for position, field in enumerate((re, im)):
                for part, piece in enumerate(split(field)):
                    begin = part * frame + position * half
                    cols_in[which, i, begin : begin + half, :] = piece
        yield
        even, odd = left_dot(which, 0, 0), left_dot(which, 1, 1)
        for i in range(2):
            mixed = even + odd if i == 0 else even - odd
            rows = slice(i * half, (i + 1) * half)
            for j in range(2):
                for part, piece in enumerate(split(mixed[:, j * half : (j + 1) * half])):
                    begin = part * frame
                    rows_in[which, j, rows, begin : begin + half] = piece[:half]
                    rows_in[which, j, rows, begin + half : begin + frame] = piece[half:]
        yield
        even, odd = right_dot(which, 0, 2), right_dot(which, 1, 3)
        total, difference = even + odd, even - odd
        for c, rows in enumerate(chunks):
            re = jnp.concatenate([total[rows, :half], difference[rows, :half]], 1)
            im = jnp.concatenate([total[rows, half:], difference[rows, half:]], 1)
            after(c, rows, re, im)

    def frames(steps_of, then=None, at_once=False):
        def group(number, nothing):
            running = [steps_of(which, number * GROUP + which) for which in range(GROUP)]
            while running:
                running = [steps for steps in running if next(steps, steps_end) is not steps_end]
            if then is not None:
                then(number)
            return nothing

        if at_once:
            running = [steps_of(which, which) for which in range(cap)]
            while running:
                running = [steps for steps in running if next(steps, steps_end) is not steps_end]
        else:
            lax.fori_loop(0, cap // GROUP, group, 0)

    wait_recv(rows_b[:4])
    start(corners_b + rows_b[4:])
    wait_recv(rows_a[4:] + cols_a + corners_a)
    for copy in inner[0]:
        copy.wait()

    def enter(which, slot):
        def before(chunk, rows):
            return times(probe[0, rows], probe[1, rows], window(pad_one, slot, 0, chunk), window(pad_one, slot, 1, chunk))

        def between(rows, re, im):
            return times(wave[0, rows], wave[1, rows], re, im)

        def after(chunk, rows, re, im):
            carry[slot, 0, rows] = re
            carry[slot, 1, rows] = im

        return there_and_back(which, before, between, after)

    frames(enter)

    wait_recv(rows_b[4:] + cols_b + corners_b)
    for copy in inner[1]:
        copy.wait()

    def leave(which, slot):
        def before(chunk, rows):
            second[slot, 0, rows] = window(pad_two, slot, 0, chunk)
            second[slot, 1, rows] = window(pad_two, slot, 1, chunk)
            return times(carry[slot, 0, rows], carry[slot, 1, rows], second[slot, 0, rows], second[slot, 1, rows])

        def between(rows, re, im):
            misfit = re * re + im * im - measured[slot, rows]
            return misfit * re, misfit * im

        def after(chunk, rows, re, im):
            two_re, two_im = conj_times(carry[slot, 0, rows], carry[slot, 1, rows], re, im)
            put(place_two, slot, 0, chunk, two_re)
            put(place_two, slot, 1, chunk, two_im)
            gexit[slot, 0, rows] = re
            gexit[slot, 1, rows] = im

        return there_and_back(which, before, between, after)

    frames(leave, at_once=True)

    blocks = ext // half
    last = blocks - 1

    def gathered(which, comp, row_block, col_block):
        target = slices[which][1]
        value = None
        for slot in range(cap):
            block, _ = column_of(slot)
            moved = col_block - block
            taken = jnp.where(jnp.logical_and(moved >= 0, moved <= 2), moved, 3)
            begin = jnp.clip(row_block * half - offsets[0, slot] + half, 0, 3 * half)
            piece = target[comp, slot, taken, pl.ds(begin, half), :]
            value = piece if value is None else value + piece
        return value

    def block_at(number):
        return pl.ds(pl.multiple_of(number * half, half), half)

    def gather_top(which, edge, first_col, step_col):
        top = slices[which][2]

        def step(number, nothing):
            col_block = first_col + number * step_col
            for comp in range(2):
                top[comp, edge, :, block_at(col_block)] = gathered(which, comp, edge * last, col_block)
            return nothing

        lax.fori_loop(0, 2, step, 0)

    def gather_sides(which):
        side = slices[which][3]

        def step(number, nothing):
            near, row_block = number % 2, number // 2
            for comp in range(2):
                side[comp, near, block_at(row_block), :] = gathered(which, comp, row_block + 1, near * last)
            return nothing

        lax.fori_loop(0, 2 * (blocks - 2), step, 0)

    def gather_inner(which):
        def step(number, nothing):
            row_block, col_block = number // (blocks - 2), number % (blocks - 2)
            for comp in range(2):
                out[2 * which + comp, block_at(row_block), block_at(col_block)] = gathered(
                    which, comp, row_block + 1, col_block + 1
                )
            return nothing

        lax.fori_loop(0, (blocks - 2) * (blocks - 2), step, 0)

    def send_sums(which):
        rows, cols, corners = folds[which]
        for edge in range(2):
            gather_top(which, edge, 2, 1)
            start(rows[4 + edge : 5 + edge])
        for edge in range(2):
            gather_top(which, edge, 0, last)
            start(corners[2 * edge : 2 * edge + 2])
        for edge in range(2):
            gather_top(which, edge, 1, last - 2)
        gather_sides(which)
        start(cols)
        gather_inner(which)

    def pass_corners(which):
        rows, _, corners = folds[which]
        _, _, top, _, _, land_cols = slices[which]
        wait_recv(corners)
        for edge, band, there in ((0, slice(0, low), has_up), (1, slice(high, ext), has_down)):
            for side, near, cell in ((0, has_left, slice(low, low + half)), (1, has_right, slice(high - half, high))):

                @pl.when(jnp.logical_and(there, near))
                def _():
                    for comp in range(2):
                        top[comp, edge, :, cell] += land_cols[side, comp, band, :]

        start(rows[:4])

    def finish(which):
        rows, cols, _ = folds[which]
        _, _, _, _, land_rows, land_cols = slices[which]
        wait_recv(cols)
        for side, near, cell in ((0, has_left, edge_pieces[0]), (1, has_right, edge_pieces[1])):

            @pl.when(near)
            def _():
                for comp in range(2):
                    out[2 * which + comp, :, cell] += land_cols[side, comp, low:high, :]

        for arrived, pieces in ((rows[4:], (middle,)), (rows[:4], edge_pieces)):
            wait_recv(arrived)
            for side, near, cell in ((0, has_up, edge_pieces[0]), (1, has_down, edge_pieces[1])):

                @pl.when(near)
                def _():
                    for comp in range(2):
                        for piece in pieces:
                            out[2 * which + comp, cell, piece] += land_rows[side, comp, :, piece]

    send_sums(1)

    def back(which, slot):
        def before(chunk, rows):
            return conj_times(second[slot, 0, rows], second[slot, 1, rows], gexit[slot, 0, rows], gexit[slot, 1, rows])

        def between(rows, re, im):
            return conj_times(wave[0, rows], wave[1, rows], re, im)

        def after(chunk, rows, re, im):
            one_re, one_im = conj_times(probe[0, rows], probe[1, rows], re, im)
            put(place_one, slot, 0, chunk, one_re)
            put(place_one, slot, 1, chunk, one_im)

        return there_and_back(which, before, between, after)

    def between_groups(number):
        @pl.when(number == 0)
        def _():
            pass_corners(1)

    frames(back, between_groups)

    send_sums(0)
    pass_corners(0)
    finish(1)
    wait_send(rows_a[4:] + cols_a + corners_a + rows_b + cols_b + corners_b)
    for copies in (*folds[1], folds[0][0][4:], *folds[0][1:]):
        wait_send(copies)
    finish(0)
    wait_send(folds[0][0][:4])


def shards(n_gx, n_gy, objects, probe_wave, prop_phase, intensity, offsets, counts):
    frame = intensity.shape[1]
    half = frame // 2
    cap = intensity.shape[0]
    tile = objects.shape[1]
    ext = tile + frame
    anywhere = pl.BlockSpec(memory_space=pl.ANY)
    field = pltpu.VMEM((cap, 2, frame, frame), F32)
    scratch = [
        *[pltpu.VMEM((2, ext // half, ext, half), F32)] * 2,
        *[pltpu.VMEM((2, cap, 4, 4 * half, half), F32)] * 2,
        *[pltpu.VMEM((2, 2, half, ext), F32)] * 2,
        *[pltpu.VMEM((2, 2, tile, half), F32)] * 2,
        *[pltpu.VMEM((2, 2, half, tile), F32)] * 2,
        *[pltpu.VMEM((2, 2, ext, half), F32)] * 2,
        field,
        field,
        field,
        pltpu.VMEM((2, frame, frame), F32),
        pltpu.VMEM((2, frame, frame), F32),
        pltpu.VMEM((cap, frame, frame), F32),
        pltpu.VMEM((6, half, half), F32),
        pltpu.VMEM((frame, frame), F32),
        pltpu.VMEM((4, 3 * frame, frame), BF16),
        pltpu.VMEM((4, frame, 3 * frame), BF16),
        pltpu.VMEM((cap, 2, frame, 2 * frame), BF16),
        pltpu.VMEM((cap, 2, 2 * frame, frame), BF16),
        pltpu.SMEM((2, cap), jnp.int32),
        pltpu.SMEM((1,), jnp.int32),
        pltpu.SemaphoreType.DMA((4 * COPIES,)),
        pltpu.SemaphoreType.DMA((4 * COPIES,)),
        pltpu.SemaphoreType.DMA((8,)),
        pltpu.SemaphoreType.DMA((2, tile // half)),
    ]
    return pl.pallas_call(
        functools.partial(kernel, n_gx, n_gy),
        out_shape=pltpu.VMEM(objects.shape, F32),
        in_specs=[anywhere] * 7,
        out_specs=pl.BlockSpec(memory_space=pltpu.VMEM),
        scratch_shapes=scratch,
        compiler_params=pltpu.CompilerParams(
            collective_id=0, has_side_effects=True, vmem_limit_bytes=58 * 1024 * 1024
        ),
        name="ptychography",
    )(offsets.T, counts, objects, probe_wave, prop_phase, intensity, jnp.asarray(phase_tables(frame)))


def solution(mesh):
    return jax.shard_map(
        functools.partial(shards, mesh.shape["gx"], mesh.shape["gy"]),
        mesh=mesh,
        in_specs=(
            P(None, "gx", "gy"),
            P(),
            P(),
            P(("gx", "gy"), None, None),
            P(("gx", "gy"), None),
            P(("gx", "gy")),
        ),
        out_specs=P(None, "gx", "gy"),
        check_vma=False,
    )
```

```python
import functools

import jax
import jax.numpy as jnp
import numpy as np
from jax import lax
from jax.experimental import pallas as pl
from jax.experimental.pallas import tpu as pltpu
from jax.sharding import PartitionSpec as P

F32 = jnp.float32
BF16 = jnp.bfloat16
MESH = pl.DeviceIdType.MESH
CHUNK = 64
COPIES = 14
GROUP = 2
steps_end = object()


def phase_tables(frame_len):
    half = frame_len // 2
    n = np.arange(half)[:, None]
    k = np.arange(half)[None, :]
    factor = 1.0 / np.sqrt(frame_len)
    even = 2.0 * np.pi * (n * 2 * k % frame_len) / frame_len
    odd = 2.0 * np.pi * (n * (2 * k + 1) % frame_len) / frame_len
    parts = [np.cos(even), np.sin(even), np.cos(odd), np.sin(odd), np.cos(odd).T, np.sin(odd).T]
    return np.stack([part * factor for part in parts]).astype(np.float32)


def split(value):
    high = value.astype(BF16)
    return high, (value - high.astype(F32)).astype(BF16)


def dot(left, right):
    return jnp.dot(left, right, preferred_element_type=F32)


def times(left_re, left_im, right_re, right_im):
    return left_re * right_re - left_im * right_im, left_re * right_im + left_im * right_re


def conj_times(left_re, left_im, right_re, right_im):
    return left_re * right_re + left_im * right_im, left_re * right_im - left_im * right_re


def kernel(
    n_gx, n_gy, offsets_hbm, counts_hbm, objects, probe_hbm, phase_hbm, intensity_hbm, tables_hbm, out,
    pad_one, pad_two, place_one, place_two, top_one, top_two, side_one, side_two, rows_one, rows_two, cols_one, cols_two,
    carry, second, gexit, probe, wave, measured, tables, phase, weights_r, weights_l, rows_in, cols_in,
    offsets, counts, send_sem, recv_sem, local_sem, inner_sem,
):
    frame = probe.shape[1]
    half = frame // 2
    cap = intensity_hbm.shape[0]
    tile = objects.shape[1]
    ext = tile + frame
    low, high = half, half + tile
    gx, gy = lax.axis_index("gx"), lax.axis_index("gy")
    has_up, has_down = gx > 0, gx < n_gx - 1
    has_left, has_right = gy > 0, gy < n_gy - 1
    up, down, left, right = (gx - 1, gy), (gx + 1, gy), (gx, gy - 1), (gx, gy + 1)
    slices = (
        (pad_one, place_one, top_one, side_one, rows_one, cols_one),
        (pad_two, place_two, top_two, side_two, rows_two, cols_two),
    )

    barrier = pltpu.get_barrier_semaphore()
    sides = ((has_up, up), (has_down, down), (has_left, left), (has_right, right))
    for there, device in sides:

        @pl.when(there)
        def _():
            pl.semaphore_signal(barrier, inc=1, device_id=device, device_id_type=MESH)

    local = [
        pltpu.make_async_copy(tables_hbm, tables, local_sem.at[0]),
        pltpu.make_async_copy(phase_hbm, phase, local_sem.at[1]),
        pltpu.make_async_copy(intensity_hbm, measured, local_sem.at[2]),
        pltpu.make_async_copy(probe_hbm, probe, local_sem.at[3]),
        pltpu.make_async_copy(offsets_hbm, offsets, local_sem.at[4]),
        pltpu.make_async_copy(counts_hbm, counts, local_sem.at[5]),
    ]
    inner = [
        [
            pltpu.make_async_copy(
                objects.at[2 * which : 2 * which + 2, :, block * half : (block + 1) * half],
                pad.at[:, block + 1, low:high],
                inner_sem.at[which, block],
            )
            for block in range(tile // half)
        ]
        for which, pad in enumerate((pad_one, pad_two))
    ]
    local += inner[0] + inner[1]
    for copy in local[:3]:
        copy.start()

    pl.semaphore_wait(barrier, sum(there.astype(jnp.int32) for there, _ in sides))

    def remote(number, source, target, device, sends, receives):
        copy = pltpu.make_async_remote_copy(
            src_ref=source, dst_ref=target, send_sem=send_sem.at[number], recv_sem=recv_sem.at[number],
            device_id=device, device_id_type=MESH,
        )
        return sends, receives, copy

    def start(copies):
        for sends, _, copy in copies:
            pl.when(sends)(copy.start)

    def wait_recv(copies):
        for _, receives, copy in copies:
            pl.when(receives)(copy.wait_recv)

    def wait_send(copies):
        for sends, _, copy in copies:
            pl.when(sends)(copy.wait_send)

    edge_pieces = (slice(0, half), slice(tile - half, tile))
    middle = slice(half, tile - half)

    def shift_by(piece, distance):
        return slice(piece.start + distance, piece.stop + distance)

    def halo(which):
        pad = slices[which][0]
        cells = objects.at[2 * which : 2 * which + 2]
        base = which * COPIES
        rows = []
        blocks = tile // half
        for block in (0, blocks - 1, *range(1, blocks - 1)):
            piece = slice(block * half, (block + 1) * half)
            rows.append(
                remote(base + len(rows), cells.at[:, 0:half, piece], pad.at[:, block + 1, high:ext], up, has_up, has_down)
            )
            rows.append(
                remote(base + len(rows), cells.at[:, tile - half : tile, piece], pad.at[:, block + 1, 0:low], down, has_down, has_up)
            )
        cols = [
            remote(base + 8, cells.at[:, :, 0:half], pad.at[:, blocks + 1, low:high], left, has_left, has_right),
            remote(base + 9, cells.at[:, :, tile - half : tile], pad.at[:, 0, low:high], right, has_right, has_left),
        ]
        corners = []
        for band, there in ((slice(0, low), has_up), (slice(high, ext), has_down)):
            to_left, to_right = jnp.logical_and(there, has_left), jnp.logical_and(there, has_right)
            corners.append(
                remote(base + 10 + len(corners), pad.at[:, 1, band], pad.at[:, blocks + 1, band], left, to_left, to_right)
            )
            corners.append(
                remote(base + 10 + len(corners), pad.at[:, blocks, band], pad.at[:, 0, band], right, to_right, to_left)
            )
        return rows, cols, corners

    def fold(which):
        _, _, top, side, land_rows, land_cols = slices[which]
        base = (2 + which) * COPIES
        rows = []
        for piece in (*edge_pieces, middle):
            moved = shift_by(piece, half)
            rows.append(
                remote(base + len(rows), top.at[:, 0, :, moved], land_rows.at[1, :, :, piece], up, has_up, has_down)
            )
            rows.append(
                remote(base + len(rows), top.at[:, 1, :, moved], land_rows.at[0, :, :, piece], down, has_down, has_up)
            )
        cols = [
            remote(base + 6, side.at[:, 0], land_cols.at[1, :, low:high], left, has_left, has_right),
            remote(base + 7, side.at[:, 1], land_cols.at[0, :, low:high], right, has_right, has_left),
        ]
        corners = []
        for edge, band, there in ((0, slice(0, low), has_up), (1, slice(high, ext), has_down)):
            to_left, to_right = jnp.logical_and(there, has_left), jnp.logical_and(there, has_right)
            corners.append(
                remote(base + 8 + len(corners), top.at[:, edge, :, 0:low], land_cols.at[1, :, band], left, to_left, to_right)
            )
            corners.append(
                remote(base + 8 + len(corners), top.at[:, edge, :, high:ext], land_cols.at[0, :, band], right, to_right, to_left)
            )
        return rows, cols, corners

    halos = [halo(0), halo(1)]
    folds = [fold(0), fold(1)]

    (rows_a, cols_a, corners_a), (rows_b, cols_b, corners_b) = halos
    start(rows_a[:4] + rows_b[:4] + cols_a)
    for copy in local[3:]:
        copy.start()

    for pad in (pad_one, pad_two):

        @pl.when(jnp.logical_not(has_up))
        def _():
            pad[:, :, 0:low] = jnp.zeros((2, ext // half, low, half), F32)

        @pl.when(jnp.logical_not(has_down))
        def _():
            pad[:, :, high:ext] = jnp.zeros((2, ext // half, low, half), F32)

        @pl.when(jnp.logical_not(has_left))
        def _():
            pad[:, 0] = jnp.zeros((2, ext, half), F32)

        @pl.when(jnp.logical_not(has_right))
        def _():
            pad[:, ext // half - 1] = jnp.zeros((2, ext, half), F32)

    local[0].wait()
    cos_e, sin_e, cos_o, sin_o, cos_t, sin_t = (tables[i] for i in range(6))

    def real_form(cosine, sine):
        return jnp.concatenate([jnp.concatenate([cosine, -sine], 1), jnp.concatenate([sine, cosine], 1)], 0)

    forms = (real_form(cos_e, sin_e), real_form(cos_o, sin_o), real_form(cos_e, -sin_e), real_form(cos_t, -sin_t))
    for number, form in enumerate(forms):
        top, rest = split(form)
        for part, value in enumerate((top, top, rest)):
            weights_r[number, part * frame : (part + 1) * frame, :] = value
            weights_l[number, :, part * frame : (part + 1) * frame] = value

    place = lax.broadcasted_iota(jnp.int32, (frame, frame), 0)
    other = lax.broadcasted_iota(jnp.int32, (frame, frame), 1)

    def picked(i):
        return jnp.where(i < half, 2 * i, 2 * (i - half) + 1)

    pick_rows = jnp.where(other == picked(place), 1.0, 0.0).astype(BF16)
    pick_cols = jnp.where(place == picked(other), 1.0, 0.0).astype(BF16)

    def sorted_frequencies(value):
        for axis in (0, 1):
            top, rest = split(value)
            middle_part, last = split(value - top.astype(F32))
            del rest
            parts = (top, middle_part, last)
            if axis == 0:
                value = sum(dot(pick_rows, part) for part in parts[::-1])
            else:
                value = sum(dot(part, pick_cols) for part in parts[::-1])
        return value

    local[1].wait()
    angle = sorted_frequencies(phase[...])
    wave[0] = jnp.cos(angle)
    wave[1] = jnp.sin(angle)
    wait_send(rows_a[:4])
    start(rows_a[4:] + cols_b)
    local[2].wait()

    def sort_slot(slot, nothing):
        measured[slot] = sorted_frequencies(measured[slot])
        return nothing

    lax.fori_loop(0, cap, sort_slot, 0)

    wait_recv(rows_a[:4])
    start(corners_a)

    def clear_place(slot, nothing):
        for target in (place_one, place_two):
            for comp in range(2):
                target[comp, slot, 3] = jnp.zeros((4 * half, half), F32)
                for block in range(3):
                    target[comp, slot, block, 0:half] = jnp.zeros((half, half), F32)
                    target[comp, slot, block, 3 * half : 4 * half] = jnp.zeros((half, half), F32)
        return nothing

    lax.fori_loop(0, cap, clear_place, 0)
    local[3].wait()
    local[4].wait()
    local[5].wait()

    lane = lax.broadcasted_iota(jnp.int32, (CHUNK, half), 1)

    def column_of(slot):
        column = offsets[1, slot]
        block = jnp.minimum(column // half, tile // half - 1)
        return block, column - block * half

    def window(pad, slot, comp, chunk):
        row = offsets[0, slot]
        block, shift = column_of(slot)
        rows = pl.ds(row + chunk * CHUNK, CHUNK)
        back = jnp.where(jnp.logical_or(shift == 0, shift == half), 0, half - shift)
        turned = [pltpu.roll(pad[comp, block + i, rows, :], back, 1) for i in range(3)]
        kept = lane < half - shift
        return jnp.concatenate([jnp.where(kept, turned[i], turned[i + 1]) for i in range(2)], 1)

    def put(target, slot, comp, chunk, value):
        _, shift = column_of(slot)
        turn = jnp.where(shift == half, 0, shift)
        value = jnp.where(slot < counts[0], value, jnp.zeros_like(value))
        first = pltpu.roll(value[:, :half], turn, 1)
        last = pltpu.roll(value[:, half:], turn, 1)
        inside = lane >= shift
        nothing = jnp.zeros_like(first)
        rows = slice(half + chunk * CHUNK, half + (chunk + 1) * CHUNK)
        target[comp, slot, 0, rows] = jnp.where(inside, first, nothing)
        target[comp, slot, 1, rows] = jnp.where(inside, last, first)
        target[comp, slot, 2, rows] = jnp.where(inside, nothing, last)

    def right_dot(lane_of, j, number):
        value = rows_in[lane_of, j]
        return dot(jnp.concatenate([value, value[:, :frame]], 1), weights_r[number])

    def left_dot(lane_of, i, number):
        value = cols_in[lane_of, i]
        return dot(weights_l[number], jnp.concatenate([value, value[:frame]], 0))

    def there_and_back(which, before, between, after):
        chunks = [slice(c * CHUNK, (c + 1) * CHUNK) for c in range(frame // CHUNK)]
        for c, rows in enumerate(chunks):
            re, im = before(c, rows)
            for j in range(2):
                if j == 0:
                    mixed = jnp.concatenate([re[:, :half] + re[:, half:], im[:, :half] + im[:, half:]], 1)
                else:
                    mixed = jnp.concatenate([re[:, :half] - re[:, half:], im[:, :half] - im[:, half:]], 1)
                top, rest = split(mixed)
                rows_in[which, j, rows, 0:frame] = top
                rows_in[which, j, rows, frame : 2 * frame] = rest
        yield
        for j in range(2):
            value = right_dot(which, j, j)
            cols = slice(j * half, (j + 1) * half)
            for i in range(2):
                mixed = value[:half] + value[half:] if i == 0 else value[:half] - value[half:]
                for part, piece in enumerate(split(mixed)):
                    cols_in[which, i, part * frame : part * frame + half, cols] = piece[:, :half]
                    cols_in[which, i, part * frame + half : (part + 1) * frame, cols] = piece[:, half:]
        yield
        for i in range(2):
            value = left_dot(which, i, 2 + i)
            re, im = between(slice(i * half, (i + 1) * half), value[:half], value[half:])
            for position, field in enumerate((re, im)):
                for part, piece in enumerate(split(field)):
                    begin = part * frame + position * half
                    cols_in[which, i, begin : begin + half, :] = piece
        yield
        even, odd = left_dot(which, 0, 0), left_dot(which, 1, 1)
        for i in range(2):
            mixed = even + odd if i == 0 else even - odd
            rows = slice(i * half, (i + 1) * half)
            for j in range(2):
                for part, piece in enumerate(split(mixed[:, j * half : (j + 1) * half])):
                    begin = part * frame
                    rows_in[which, j, rows, begin : begin + half] = piece[:half]
                    rows_in[which, j, rows, begin + half : begin + frame] = piece[half:]
        yield
        even, odd = right_dot(which, 0, 2), right_dot(which, 1, 3)
        total, difference = even + odd, even - odd
        for c, rows in enumerate(chunks):
            re = jnp.concatenate([total[rows, :half], difference[rows, :half]], 1)
            im = jnp.concatenate([total[rows, half:], difference[rows, half:]], 1)
            after(c, rows, re, im)

    def frames(steps_of, then=None, at_once=False):
        def group(number, nothing):
            running = [steps_of(which, number * GROUP + which) for which in range(GROUP)]
            while running:
                running = [steps for steps in running if next(steps, steps_end) is not steps_end]
            if then is not None:
                then(number)
            return nothing

        if at_once:
            running = [steps_of(which, which) for which in range(cap)]
            while running:
                running = [steps for steps in running if next(steps, steps_end) is not steps_end]
        else:
            lax.fori_loop(0, cap // GROUP, group, 0)

    wait_recv(rows_b[:4])
    start(corners_b + rows_b[4:])
    wait_recv(rows_a[4:] + cols_a + corners_a)
    for copy in inner[0]:
        copy.wait()

    def enter(which, slot):
        def before(chunk, rows):
            return times(probe[0, rows], probe[1, rows], window(pad_one, slot, 0, chunk), window(pad_one, slot, 1, chunk))

        def between(rows, re, im):
            return times(wave[0, rows], wave[1, rows], re, im)

        def after(chunk, rows, re, im):
            carry[slot, 0, rows] = re
            carry[slot, 1, rows] = im

        return there_and_back(which, before, between, after)

    frames(enter, at_once=True)

    wait_recv(rows_b[4:] + cols_b + corners_b)
    for copy in inner[1]:
        copy.wait()

    def leave(which, slot):
        def before(chunk, rows):
            second[slot, 0, rows] = window(pad_two, slot, 0, chunk)
            second[slot, 1, rows] = window(pad_two, slot, 1, chunk)
            return times(carry[slot, 0, rows], carry[slot, 1, rows], second[slot, 0, rows], second[slot, 1, rows])

        def between(rows, re, im):
            misfit = re * re + im * im - measured[slot, rows]
            return misfit * re, misfit * im

        def after(chunk, rows, re, im):
            two_re, two_im = conj_times(carry[slot, 0, rows], carry[slot, 1, rows], re, im)
            put(place_two, slot, 0, chunk, two_re)
            put(place_two, slot, 1, chunk, two_im)
            gexit[slot, 0, rows] = re
            gexit[slot, 1, rows] = im

        return there_and_back(which, before, between, after)

    frames(leave, at_once=True)

    blocks = ext // half
    last = blocks - 1

    def gathered(which, comp, row_block, col_block):
        target = slices[which][1]
        value = None
        for slot in range(cap):
            block, _ = column_of(slot)
            moved = col_block - block
            taken = jnp.where(jnp.logical_and(moved >= 0, moved <= 2), moved, 3)
            begin = jnp.clip(row_block * half - offsets[0, slot] + half, 0, 3 * half)
            piece = target[comp, slot, taken, pl.ds(begin, half), :]
            value = piece if value is None else value + piece
        return value

    def block_at(number):
        return pl.ds(pl.multiple_of(number * half, half), half)

    def gather_top(which, edge, first_col, step_col):
        top = slices[which][2]

        def step(number, nothing):
            col_block = first_col + number * step_col
            for comp in range(2):
                top[comp, edge, :, block_at(col_block)] = gathered(which, comp, edge * last, col_block)
            return nothing

        lax.fori_loop(0, 2, step, 0)

    def gather_sides(which):
        side = slices[which][3]

        def step(number, nothing):
            near, row_block = number % 2, number // 2
            for comp in range(2):
                side[comp, near, block_at(row_block), :] = gathered(which, comp, row_block + 1, near * last)
            return nothing

        lax.fori_loop(0, 2 * (blocks - 2), step, 0)

    def gather_inner(which):
        def step(number, nothing):
            row_block, col_block = number // (blocks - 2), number % (blocks - 2)
            for comp in range(2):
                out[2 * which + comp, block_at(row_block), block_at(col_block)] = gathered(
                    which, comp, row_block + 1, col_block + 1
                )
            return nothing

        lax.fori_loop(0, (blocks - 2) * (blocks - 2), step, 0)

    def send_sums(which):
        rows, cols, corners = folds[which]
        for edge in range(2):
            gather_top(which, edge, 2, 1)
            start(rows[4 + edge : 5 + edge])
        for edge in range(2):
            gather_top(which, edge, 0, last)
            start(corners[2 * edge : 2 * edge + 2])
        for edge in range(2):
            gather_top(which, edge, 1, last - 2)
        gather_sides(which)
        start(cols)
        gather_inner(which)

    def pass_corners(which):
        rows, _, corners = folds[which]
        _, _, top, _, _, land_cols = slices[which]
        wait_recv(corners)
        for edge, band, there in ((0, slice(0, low), has_up), (1, slice(high, ext), has_down)):
            for side, near, cell in ((0, has_left, slice(low, low + half)), (1, has_right, slice(high - half, high))):

                @pl.when(jnp.logical_and(there, near))
                def _():
                    for comp in range(2):
                        top[comp, edge, :, cell] += land_cols[side, comp, band, :]

        start(rows[:4])

    def finish(which):
        rows, cols, _ = folds[which]
        _, _, _, _, land_rows, land_cols = slices[which]
        wait_recv(cols)
        for side, near, cell in ((0, has_left, edge_pieces[0]), (1, has_right, edge_pieces[1])):

            @pl.when(near)
            def _():
                for comp in range(2):
                    out[2 * which + comp, :, cell] += land_cols[side, comp, low:high, :]

        for arrived, pieces in ((rows[4:], (middle,)), (rows[:4], edge_pieces)):
            wait_recv(arrived)
            for side, near, cell in ((0, has_up, edge_pieces[0]), (1, has_down, edge_pieces[1])):

                @pl.when(near)
                def _():
                    for comp in range(2):
                        for piece in pieces:
                            out[2 * which + comp, cell, piece] += land_rows[side, comp, :, piece]

    send_sums(1)

    def back(which, slot):
        def before(chunk, rows):
            return conj_times(second[slot, 0, rows], second[slot, 1, rows], gexit[slot, 0, rows], gexit[slot, 1, rows])

        def between(rows, re, im):
            return conj_times(wave[0, rows], wave[1, rows], re, im)

        def after(chunk, rows, re, im):
            one_re, one_im = conj_times(probe[0, rows], probe[1, rows], re, im)
            put(place_one, slot, 0, chunk, one_re)
            put(place_one, slot, 1, chunk, one_im)

        return there_and_back(which, before, between, after)

    def between_groups(number):
        @pl.when(number == 0)
        def _():
            pass_corners(1)

    frames(back, between_groups)

    send_sums(0)
    pass_corners(0)
    finish(1)
    wait_send(rows_a[4:] + cols_a + corners_a + rows_b + cols_b + corners_b)
    for copies in (*folds[1], folds[0][0][4:], *folds[0][1:]):
        wait_send(copies)
    finish(0)
    wait_send(folds[0][0][:4])


def shards(n_gx, n_gy, objects, probe_wave, prop_phase, intensity, offsets, counts):
    frame = intensity.shape[1]
    half = frame // 2
    cap = intensity.shape[0]
    tile = objects.shape[1]
    ext = tile + frame
    anywhere = pl.BlockSpec(memory_space=pl.ANY)
    field = pltpu.VMEM((cap, 2, frame, frame), F32)
    scratch = [
        *[pltpu.VMEM((2, ext // half, ext, half), F32)] * 2,
        *[pltpu.VMEM((2, cap, 4, 4 * half, half), F32)] * 2,
        *[pltpu.VMEM((2, 2, half, ext), F32)] * 2,
        *[pltpu.VMEM((2, 2, tile, half), F32)] * 2,
        *[pltpu.VMEM((2, 2, half, tile), F32)] * 2,
        *[pltpu.VMEM((2, 2, ext, half), F32)] * 2,
        field,
        field,
        field,
        pltpu.VMEM((2, frame, frame), F32),
        pltpu.VMEM((2, frame, frame), F32),
        pltpu.VMEM((cap, frame, frame), F32),
        pltpu.VMEM((6, half, half), F32),
        pltpu.VMEM((frame, frame), F32),
        pltpu.VMEM((4, 3 * frame, frame), BF16),
        pltpu.VMEM((4, frame, 3 * frame), BF16),
        pltpu.VMEM((cap, 2, frame, 2 * frame), BF16),
        pltpu.VMEM((cap, 2, 2 * frame, frame), BF16),
        pltpu.SMEM((2, cap), jnp.int32),
        pltpu.SMEM((1,), jnp.int32),
        pltpu.SemaphoreType.DMA((4 * COPIES,)),
        pltpu.SemaphoreType.DMA((4 * COPIES,)),
        pltpu.SemaphoreType.DMA((8,)),
        pltpu.SemaphoreType.DMA((2, tile // half)),
    ]
    return pl.pallas_call(
        functools.partial(kernel, n_gx, n_gy),
        out_shape=pltpu.VMEM(objects.shape, F32),
        in_specs=[anywhere] * 7,
        out_specs=pl.BlockSpec(memory_space=pltpu.VMEM),
        scratch_shapes=scratch,
        compiler_params=pltpu.CompilerParams(
            collective_id=0, has_side_effects=True, vmem_limit_bytes=58 * 1024 * 1024
        ),
        name="ptychography",
    )(offsets.T, counts, objects, probe_wave, prop_phase, intensity, jnp.asarray(phase_tables(frame)))


def solution(mesh):
    return jax.shard_map(
        functools.partial(shards, mesh.shape["gx"], mesh.shape["gy"]),
        mesh=mesh,
        in_specs=(
            P(None, "gx", "gy"),
            P(),
            P(),
            P(("gx", "gy"), None, None),
            P(("gx", "gy"), None),
            P(("gx", "gy")),
        ),
        out_specs=P(None, "gx", "gy"),
        check_vma=False,
    )
```
